32 devices in a mesh: row: 4 (over z), col: 8 (over y, x, core).
Axes of the slice: x: 2, y: 2, z: 4, core: 2. Of those that a mesh axis runs over, the one named last changes fastest.
Arguments:
- points: bfloat16 [2, 8192], P(None, ('row', 'col')), may hold values from 0 to 1
- noise_var: float32 [8192], P(('row', 'col')), may hold values from 0.5 to 2
- district: int32 [8192], P(('row', 'col')), may hold values from 0 to 63, never falling along the last dimension, each value on 1 to 512 neighbouring positions
- solution: float32 [32, 8192], P(None, ('row', 'col')), may hold values from -6 to 6
- residual: float32 [32, 8192], P(None, ('row', 'col')), may hold values from -44 to 44
- direction: float32 [32, 8192], P(None, ('row', 'col')), may hold values from -44 to 44
Outputs:
- new_solution: float32 [32, 8192], P(None, ('row', 'col'))
- new_residual: float32 [32, 8192], P(None, ('row', 'col'))
- new_direction: float32 [32, 8192], P(None, ('row', 'col'))
The draws below stay inside these ranges and needn't reach their ends.
Inputs may be any that keep to these rules, and one draw needn't show every extreme that they name: Samples are ordered by district; every district holds 1 to 512 samples and one holds exactly 512.
All inputs are finite; a program needn't handle non-finite values.
Results may differ from the reference program's by a relative error of at most 0.004.
Values may be sent and summed in bfloat16 or wider, within the bound.
No kernel may reach another device: no remote copies, remote signals or barrier semaphores. Data moves between devices by JAX's collectives and lax.ppermute only.
A program may use at most 64 MiB of HBM per device.

```python
import math
import jax
import jax.numpy as jnp
import numpy as np
from jax import lax

NRHS = 32
NDIST = 64
SAMPLES = 8192
DIST_MOST = 512


def profile_draw(key):
    key_rough, key_scale, key_base = jax.random.split(key, 3)
    ramp = 0.6 + 1.2 * jnp.arange(SAMPLES, dtype=jnp.float32) / SAMPLES
    rough = jax.random.uniform(key_rough, (SAMPLES,), jnp.float32, 0.5, 2.0)
    rhs_scale = jnp.exp(jax.random.uniform(key_scale, (NRHS, 1), jnp.float32, jnp.log(0.3), jnp.log(3.0)))
    base = jax.random.normal(key_base, (NRHS, SAMPLES), jnp.float32)
    base = jnp.clip(base, -4.0, 4.0)
    return base * rhs_scale * ramp[None, :] * rough[None, :]


def draw_points(key, part):
    key_drawn = jax.random.fold_in(jax.random.fold_in(key, 37), 0)
    drawn_points = jax.random.uniform(key_drawn, (2, SAMPLES), jnp.float32, 0.0, 1.0)
    result = drawn_points
    return result.astype(jnp.bfloat16)


def draw_residual(key, part):
    return profile_draw(jax.random.fold_in(key, 11))


def draw_direction(key, part):
    return profile_draw(jax.random.fold_in(key, 23))


def shard_levels(stream_key, shape, cuts, smallest, largest):
    def one(position, parts):
        draws = jax.random.uniform(jax.random.fold_in(jax.random.fold_in(stream_key, 6), position), (parts,), jnp.float32, smallest / len(cuts), largest / len(cuts))
        return jnp.repeat(jnp.exp(draws), shape[position] // parts).reshape((-1,) + (1,) * (len(shape) - position - 1))

    loudness = one(*cuts[0])
    for cut in cuts[1:]:
        loudness = loudness * one(*cut)
    return loudness


def profile(number_of, total, most, skew):
    weights = [(1 << 20) // math.isqrt(grade ** skew) + 1 for grade in range(2, number_of + 1)]
    surplus, counts = total - most - (number_of - 1), [1] * (number_of - 1)
    while surplus > 0:
        free = [i for i in range(number_of - 1) if counts[i] < most]
        mass, budget = sum([weights[i] for i in free]), surplus
        for i in free:
            addition = min(most - counts[i], max(1, budget * weights[i] // mass), surplus)
            counts[i] = counts[i] + addition
            surplus = surplus - addition
    return np.array([most] + counts)


def ragged(own_key, amount, total, most, skew):
    if amount == 2:
        one = jax.random.randint(own_key, (), max(1, total - most), min(most, total - 1) + 1)
        return jnp.stack([one, total - one])
    sizes = jnp.asarray(profile(amount, total, most, skew), jnp.int32)
    pairs = (amount - 1) // 2
    giver, taker = sizes[1:1 + 2 * pairs:2], sizes[2:2 + 2 * pairs:2]
    slack = jnp.minimum(giver - 1, most - taker)
    moved = jax.random.randint(jax.random.fold_in(own_key, 1), (pairs,), 0, 1 << 20) % (slack + 1)
    sizes = sizes.at[1:1 + 2 * pairs:2].set(giver - moved).at[2:2 + 2 * pairs:2].set(taker + moved)
    return sizes[jax.random.permutation(jax.random.fold_in(own_key, 2), amount)]


def scatter_about(key, extent, scale, bound, shards=(), kind=jnp.bfloat16):
    drawn = jax.random.normal(key, extent, jnp.float32) * scale
    if len(shards) > 0:
        drawn = shard_levels(key, extent, shards, -0.22, 0.18) * drawn
    return jnp.clip(drawn, min=-bound, max=bound).astype(kind)


def setup_inputs(seed: int = 0) -> dict:
    key_of = jax.random.split(jax.random.key(seed), 7)
    return {
        "points": draw_points(jax.random.fold_in(key_of[6], 71), 0),
        "noise_var": jnp.clip(jnp.exp(math.log(2.0) - 1.3862944 * jax.random.uniform(key_of[1], (SAMPLES,), jnp.float32) ** shard_levels(key_of[1], (SAMPLES,), ((0, 32),), -0.2, 0.2)), 0.5, 2.0),
        "district": jnp.searchsorted(jnp.cumsum(ragged(key_of[2], NDIST, SAMPLES, DIST_MOST, 2)), jnp.arange(SAMPLES), side="right").astype(jnp.int32),
        "solution": scatter_about(key_of[3], (NRHS, SAMPLES), 1.0, 6.0, ((1, 32),), jnp.float32),
        "residual": draw_residual(jax.random.fold_in(key_of[6], 71), 0),
        "direction": draw_direction(jax.random.fold_in(key_of[6], 71), 0),
    }


root_three = math.sqrt(3.0)
corr_range = 0.05
district_gain = 0.5

def matern_tile(left_points, right_points):
    left_vals = left_points.astype(jnp.float32)
    right_vals = right_points.astype(jnp.float32)
    delta_x = left_vals[0][:, None] - right_vals[0][None, :]
    delta_y = left_vals[1][:, None] - right_vals[1][None, :]
    scaled = root_three / corr_range * jnp.sqrt(delta_x * delta_x + delta_y * delta_y)
    return ((1.0 + scaled) * jnp.exp(-scaled)).astype(jnp.bfloat16)

def small_product(left, right):
    return jnp.dot(left.astype(jnp.float32), right.astype(jnp.float32), precision=lax.Precision.HIGHEST, preferred_element_type=jnp.float32)

def chol_solve(matrix, rhs_mat):
    factor = jnp.linalg.cholesky(matrix)
    return jax.scipy.linalg.cho_solve((factor, True), rhs_mat)

def reference(points, noise_var, district, solution, residual, direction):
    sizes = jax.ops.segment_sum(jnp.ones((SAMPLES,), jnp.float32), district, num_segments=NDIST)
    district_sums = jax.ops.segment_sum(direction.T, district, num_segments=NDIST).T
    lowered = direction.astype(jnp.bfloat16)
    blocks = points.reshape(2, SAMPLES // 512, 512).transpose(1, 0, 2)

    def one_block(block_points):
        return jnp.dot(lowered.astype(jnp.float32), matern_tile(points, block_points).astype(jnp.float32), preferred_element_type=jnp.float32)
    terms = lax.map(one_block, blocks)
    kernel_part = terms.transpose(1, 0, 2).reshape(NRHS, SAMPLES)
    weights = district_sums / jnp.sqrt(sizes)[None, :]
    district_part = jnp.take(weights, district, axis=1)
    kernel_scale = 1.0 / (corr_range * math.sqrt(SAMPLES))
    image = noise_var[None, :] * direction + kernel_part * kernel_scale + district_gain * district_part
    old_norm = small_product(residual, residual.T)
    curvature = small_product(direction, image.T)
    alpha = chol_solve(curvature, old_norm)
    new_solution = solution + small_product(alpha.T, direction)
    new_residual = residual - small_product(alpha.T, image)
    new_norm = small_product(new_residual, new_residual.T)
    beta = chol_solve(old_norm, new_norm)
    new_direction = new_residual + small_product(beta.T, direction)
    return (new_solution, new_residual, new_direction)
```

```python
import functools
import math

import jax
import jax.numpy as jnp
from jax import lax
from jax.experimental import pallas as pl
from jax.experimental.pallas import tpu as pltpu
from jax.sharding import Mesh, PartitionSpec as P

root_three = math.sqrt(3.0)
corr_range = 0.05
district_gain = 0.5
LANES = 128
ROWS = 72
F32, BF16 = jnp.float32, jnp.bfloat16


def dot_f32(left, right, dims):
    return lax.dot_general(
        left, right, (dims, ((), ())), precision=lax.Precision.HIGHEST, preferred_element_type=F32
    )


def dot_bf16(left, right, dims):
    return lax.dot_general(left, right, (dims, ((), ())), preferred_element_type=F32)


def three_pieces(vals):
    high = vals.astype(BF16)
    rest = vals - high.astype(F32)
    mid = rest.astype(BF16)
    low = (rest - mid.astype(F32)).astype(BF16)
    return high, mid, low


def pack_kernel(copies, points_ref, dist_ref, dir_ref, res_ref, pack_ref, own_ref, norm_ref):
    count = dir_ref.shape[1]
    rhs = dir_ref.shape[0]
    direction = dir_ref[...]
    dist = dist_ref[...]
    high, mid, low = three_pieces(direction)
    pad = jnp.zeros((LANES - 3 * rhs, count), BF16)
    ones = jnp.ones((LANES - 3 * rhs, count), BF16)
    stacked = jnp.concatenate([high, mid, low, ones], axis=0)
    labels = lax.broadcasted_iota(jnp.int32, (64, count), 0)
    onehot = (labels == dist).astype(F32).astype(BF16)
    same = dot_bf16(onehot, onehot, ((0,), (0,))).astype(BF16)
    sums = dot_bf16(stacked, same, ((1,), (0,)))
    own = sums[0:rhs] + sums[rhs : 2 * rhs] + sums[2 * rhs : 3 * rhs]
    own_ref[0:rhs, :] = own
    own_ref[rhs:, :] = sums[3 * rhs : 3 * rhs + 8]
    first = dist[:, 0:1]
    last = dist[:, count - 1 : count]
    row = lax.broadcasted_iota(jnp.int32, (8, count), 0)
    picked = jnp.where(row == 0, first, last)
    wanted = (row == 0) | ((row == 1) & (first != last))
    mask = (wanted & (dist == picked)).astype(F32).astype(BF16)
    edge = dot_bf16(mask, stacked, ((1,), (1,)))
    total = edge + pltpu.roll(edge, LANES - rhs, 1) + pltpu.roll(edge, LANES - 2 * rhs, 1)
    lane = lax.broadcasted_iota(jnp.int32, (8, LANES), 1)
    total = jnp.where(lane < rhs, total, 0.0)
    e_high, e_mid, e_low = three_pieces(total)
    row8 = lax.broadcasted_iota(jnp.int32, (8, LANES), 0)
    label = jnp.where(row8 == 0, first, last).astype(F32)
    extras = (
        e_high.astype(F32)
        + pltpu.roll(e_mid.astype(F32), rhs, 1)
        + pltpu.roll(e_low.astype(F32), 2 * rhs, 1)
    )
    extras = jnp.where(lane == 3 * rhs, label, extras)
    extras = jnp.where(lane == 3 * rhs + 1, edge, extras)
    pts = points_ref[...].astype(F32)
    tail = jnp.concatenate(
        [pts[:, 0:LANES], pts[:, LANES:], extras[0:2, :], jnp.zeros((2, LANES), F32)], axis=0
    )
    lowered = direction.astype(BF16)
    block = jnp.concatenate(
        [lowered[:, 0:LANES].astype(F32), lowered[:, LANES:].astype(F32), tail], axis=0
    ).astype(BF16)
    for n in range(copies):
        pack_ref[n] = block
    norm_ref[...] = dot_f32(res_ref[...], res_ref[...], ((1,), (1,)))


def pack(copies, points, district, direction, residual):
    rhs, count = direction.shape
    return pl.pallas_call(
        functools.partial(pack_kernel, copies),
        out_shape=(
            jax.ShapeDtypeStruct((copies, ROWS, LANES), BF16),
            jax.ShapeDtypeStruct((rhs + 8, count), F32),
            jax.ShapeDtypeStruct((rhs, rhs), F32),
        ),
        name="pack",
    )(points, district.reshape(1, count), direction, residual)


def half_product(skip, points_ref, dist_ref, all_ref, own_x, own_y):
    blocks = all_ref.shape[0]
    count = dist_ref.shape[1]
    rhs = 32
    scale = root_three / corr_range
    pts = points_ref[...].astype(BF16)
    row = lax.broadcasted_iota(jnp.int32, (2, LANES), 0)
    own_x[...] = dot_bf16(pts, (row == 0).astype(F32).astype(BF16), ((0,), (0,))) * scale
    own_y[...] = dot_bf16(pts, (row == 1).astype(F32).astype(BF16), ((0,), (0,))) * scale

    def one_block(index, acc):
        block = all_ref[index]
        tail = block[64:72, :].astype(F32) * scale
        halves = []
        for half in range(2):
            right_x = tail[2 * half : 2 * half + 1, :]
            right_y = tail[2 * half + 1 : 2 * half + 2, :]
            parts = []
            step = 64
            for start in range(0, count, step):
                dx = own_x[start : start + step, :] - right_x
                dy = own_y[start : start + step, :] - right_y
                square = jnp.maximum(dx * dx + dy * dy, 1e-30)
                scaled = square * lax.rsqrt(square)
                parts.append(((1.0 + scaled) * jnp.exp(-scaled)).astype(BF16))
            halves.append(jnp.concatenate(parts, axis=0))
        tile = jnp.concatenate(halves, axis=1)
        left = jnp.concatenate([block[0:rhs, :], block[rhs : 2 * rhs, :]], axis=1)
        return acc + dot_bf16(left, tile, ((1,), (1,)))

    product = lax.fori_loop(0, blocks, one_block, jnp.zeros((rhs, count), F32))

    edges = all_ref[:, 64:72, :].astype(F32).reshape(blocks * 8, LANES)
    place = lax.broadcasted_iota(jnp.int32, (blocks * 8, count), 0)
    kind = place % 8
    good = ((kind == 4) | (kind == 5)) & (place // 8 != skip)
    match = good & (edges[:, 3 * rhs : 3 * rhs + 1] == dist_ref[...].astype(F32))
    sums = dot_bf16(edges.astype(BF16), match.astype(F32).astype(BF16), ((0,), (0,)))
    extra = sums[0:rhs] + sums[rhs : 2 * rhs] + sums[2 * rhs : 3 * rhs]
    return product, extra, sums[3 * rhs : 3 * rhs + 8]


def first_kernel(where_ref, points_ref, dist_ref, own_ref, all_ref, product_ref, sums_ref, own_x, own_y):
    product, extra, number = half_product(where_ref[0], points_ref, dist_ref, all_ref, own_x, own_y)
    product_ref[...] = product
    sums_ref[0:32, :] = own_ref[0:32, :] + extra
    sums_ref[32:40, :] = own_ref[32:40, :]
    sums_ref[32:33, :] = own_ref[32:33, :] + number[1:2, :]


def second_kernel(
    whole_count, points_ref, dist_ref, noise_ref, dir_ref, res_ref, norm_ref, product_ref, sums_ref, all_ref,
    image_ref, gram_ref, own_x, own_y,
):
    product, extra, number = half_product(-1, points_ref, dist_ref, all_ref, own_x, own_y)
    product = product + product_ref[...]
    size = sums_ref[32:33, :] + number[1:2, :]
    district_part = (sums_ref[0:32, :] + extra) / jnp.sqrt(size)
    direction = dir_ref[...]
    kernel_scale = 1.0 / (corr_range * math.sqrt(whole_count))
    image = noise_ref[...] * direction + product * kernel_scale + district_gain * district_part
    image_ref[...] = image
    right = jnp.concatenate([direction, res_ref[...], image], axis=0)
    gram_ref[:, 0:96] = dot_f32(image, right, ((1,), (1,)))
    gram_ref[:, 96:128] = norm_ref[...]


def final_kernel(gram_ref, sol_ref, res_ref, dir_ref, image_ref, new_sol_ref, new_res_ref, new_dir_ref):
    rhs = 32
    total = gram_ref[0]
    for n in range(1, gram_ref.shape[0]):
        total = total + gram_ref[n]
    curv = total[:, 0:32]
    cross = total[:, 32:64]
    gram_image = total[:, 64:96]
    old_norm = total[:, 96:128]
    curv = 0.5 * (curv + curv.T)
    row = lax.broadcasted_iota(jnp.int32, (rhs, rhs), 0)
    col = lax.broadcasted_iota(jnp.int32, (rhs, rhs), 1)
    eye = (row == col).astype(F32)
    work = jnp.concatenate([curv, old_norm, old_norm, eye], axis=1)
    rows = lax.broadcasted_iota(jnp.int32, (rhs, LANES), 0)
    lanes = lax.broadcasted_iota(jnp.int32, (rhs, LANES), 1)
    left_side = lanes < 64
    for step in range(rhs):
        factor = jnp.where(left_side, work[:, step : step + 1], work[:, 64 + step : 65 + step])
        pivot_row = work[step : step + 1, :]
        pivot = jnp.where(left_side[0:1], work[step : step + 1, step : step + 1], work[step : step + 1, 64 + step : 65 + step])
        scaled_row = pivot_row / pivot
        work = jnp.where(rows == step, scaled_row, work - factor * scaled_row)
    alpha = work[:, 32:64]
    norm_inverse = work[:, 96:128]
    across = dot_f32(alpha, cross, ((0,), (0,)))
    squared = dot_f32(alpha, dot_f32(gram_image, alpha, ((1,), (0,))), ((0,), (0,)))
    new_norm = old_norm - across - across.T + squared
    beta = dot_f32(norm_inverse, new_norm, ((1,), (0,)))
    direction = dir_ref[...]
    new_sol_ref[...] = sol_ref[...] + dot_f32(alpha, direction, ((0,), (0,)))
    new_res = res_ref[...] - dot_f32(alpha, image_ref[...], ((0,), (0,)))
    new_res_ref[...] = new_res
    new_dir_ref[...] = new_res + dot_f32(beta, direction, ((0,), (0,)))


VMEM_LIMIT = 48 * 1024 * 1024


def per_device(chips, points, noise_var, district, solution, residual, direction):
    rhs, count = direction.shape
    whole_count = count * chips * 2
    group = ("row", "pair")
    swap = [(0, 1), (1, 0)]
    params = pltpu.CompilerParams(vmem_limit_bytes=VMEM_LIMIT)
    packed, own, norm = pack(chips, points, district, direction, residual)
    near = lax.all_to_all(packed, group, 0, 0)
    far = lax.ppermute(near, "side", swap)
    where = lax.axis_index(group).astype(jnp.int32).reshape(1)
    dist_row = district.reshape(1, count)
    noise_row = noise_var.reshape(1, count)
    own_scratch = [pltpu.VMEM((count, LANES), F32), pltpu.VMEM((count, LANES), F32)]
    vmem = pl.BlockSpec(memory_space=pltpu.VMEM)
    product, sums = pl.pallas_call(
        first_kernel,
        out_shape=(
            jax.ShapeDtypeStruct((rhs, count), F32),
            jax.ShapeDtypeStruct((rhs + 8, count), F32),
        ),
        in_specs=[pl.BlockSpec(memory_space=pltpu.SMEM)] + [vmem] * 4,
        out_specs=(vmem, vmem),
        scratch_shapes=own_scratch,
        compiler_params=params,
        name="near_half",
    )(where, points, dist_row, own, near)
    image, gram = pl.pallas_call(
        functools.partial(second_kernel, whole_count),
        out_shape=(
            jax.ShapeDtypeStruct((rhs, count), F32),
            jax.ShapeDtypeStruct((rhs, LANES), F32),
        ),
        in_specs=[vmem] * 9,
        out_specs=(vmem, vmem),
        scratch_shapes=own_scratch,
        compiler_params=params,
        name="far_half",
    )(points, dist_row, noise_row, direction, residual, norm, product, sums, far)
    chip_gram = gram + lax.ppermute(gram, "side", swap)
    grams = lax.all_to_all(jnp.broadcast_to(chip_gram[None], (chips, rhs, LANES)), group, 0, 0)
    return pl.pallas_call(
        final_kernel,
        out_shape=tuple(jax.ShapeDtypeStruct((rhs, count), F32) for _ in range(3)),
        in_specs=[vmem] * 5,
        out_specs=(vmem,) * 3,
        compiler_params=params,
        name="final",
    )(grams, solution, residual, direction, image)


def solution(mesh):
    rows, cols = mesh.shape["row"], mesh.shape["col"]
    paired = Mesh(mesh.devices.reshape(rows, cols // 2, 2), ("row", "pair", "side"))
    samples = ("row", "pair", "side")
    wide, flat = P(None, samples), P(samples)
    return jax.shard_map(
        functools.partial(per_device, rows * cols // 2),
        mesh=paired,
        in_specs=(wide, flat, flat, wide, wide, wide),
        out_specs=(wide, wide, wide),
        check_vma=False,
    )
```

```python
import functools
import math

import jax
import jax.numpy as jnp
from jax import lax
from jax.experimental import pallas as pl
from jax.experimental.pallas import tpu as pltpu
from jax.sharding import Mesh, PartitionSpec as P

root_three = math.sqrt(3.0)
corr_range = 0.05
district_gain = 0.5
LANES = 128
ROWS = 72
F32, BF16 = jnp.float32, jnp.bfloat16


def dot_f32(left, right, dims):
    return lax.dot_general(
        left, right, (dims, ((), ())), precision=lax.Precision.HIGHEST, preferred_element_type=F32
    )


def dot_bf16(left, right, dims):
    return lax.dot_general(left, right, (dims, ((), ())), preferred_element_type=F32)


def three_pieces(vals):
    high = vals.astype(BF16)
    rest = vals - high.astype(F32)
    mid = rest.astype(BF16)
    low = (rest - mid.astype(F32)).astype(BF16)
    return high, mid, low


def pack_kernel(points_ref, dist_ref, noise_ref, dir_ref, pack_ref, own_ref):
    rhs, count = dir_ref.shape
    direction = dir_ref[...]
    dist = dist_ref[...]
    high, mid, low = three_pieces(direction)
    ones = jnp.ones((LANES - 3 * rhs, count), BF16)
    stacked = jnp.concatenate([high, mid, low, ones], axis=0)
    labels = lax.broadcasted_iota(jnp.int32, (64, count), 0)
    onehot = (labels == dist).astype(F32).astype(BF16)
    same = dot_bf16(onehot, onehot, ((0,), (0,))).astype(BF16)
    sums = dot_bf16(stacked, same, ((1,), (0,)))
    pts = points_ref[...].astype(F32)
    own_ref[0:rhs, :] = sums[0:rhs] + sums[rhs : 2 * rhs] + sums[2 * rhs : 3 * rhs]
    own_ref[rhs:, :] = sums[3 * rhs : 3 * rhs + 8]
    own_ref[rhs + 1 : rhs + 2, :] = dist.astype(F32)
    own_ref[rhs + 2 : rhs + 3, :] = noise_ref[...]
    own_ref[rhs + 3 : rhs + 5, :] = pts
    first = dist[:, 0:1]
    last = dist[:, count - 1 : count]
    row = lax.broadcasted_iota(jnp.int32, (8, count), 0)
    picked = jnp.where(row == 0, first, last)
    wanted = (row == 0) | ((row == 1) & (first != last))
    mask = (wanted & (dist == picked)).astype(F32).astype(BF16)
    edge = dot_bf16(mask, stacked, ((1,), (1,)))
    total = edge + pltpu.roll(edge, LANES - rhs, 1) + pltpu.roll(edge, LANES - 2 * rhs, 1)
    lane = lax.broadcasted_iota(jnp.int32, (8, LANES), 1)
    total = jnp.where(lane < rhs, total, 0.0)
    e_high, e_mid, e_low = three_pieces(total)
    row8 = lax.broadcasted_iota(jnp.int32, (8, LANES), 0)
    label = jnp.where(row8 == 0, first, last).astype(F32)
    extras = (
        e_high.astype(F32)
        + pltpu.roll(e_mid.astype(F32), rhs, 1)
        + pltpu.roll(e_low.astype(F32), 2 * rhs, 1)
    )
    extras = jnp.where(lane == 3 * rhs, label, extras)
    extras = jnp.where(lane == 3 * rhs + 1, edge, extras)
    tail = jnp.concatenate(
        [pts[:, 0:LANES], pts[:, LANES:], extras[0:2, :], jnp.zeros((2, LANES), F32)], axis=0
    )
    pack_ref[0:rhs, :] = high[:, 0:LANES]
    pack_ref[rhs : 2 * rhs, :] = high[:, LANES:]
    pack_ref[2 * rhs :, :] = tail.astype(BF16)


def half_product(skip, own_ref, all_ref, own_x, own_y):
    blocks = all_ref.shape[0]
    count = own_ref.shape[1]
    rhs = 32
    scale = root_three / corr_range
    own = own_ref[rhs:, :]
    pts = own.astype(BF16)
    row = lax.broadcasted_iota(jnp.int32, (8, LANES), 0)
    own_x[...] = dot_bf16(pts, (row == 3).astype(F32).astype(BF16), ((0,), (0,))) * scale
    own_y[...] = dot_bf16(pts, (row == 4).astype(F32).astype(BF16), ((0,), (0,))) * scale
    step = 16
    to_two = -math.log2(math.e)

    def one_block(index, acc):
        block = all_ref[index]
        tail = block[2 * rhs :, :].astype(F32) * scale
        halves = []
        for half in range(2):
            right_x = tail[2 * half : 2 * half + 1, :]
            right_y = tail[2 * half + 1 : 2 * half + 2, :]
            parts = []
            for start in range(0, count, step):
                dx = own_x[start : start + step, :] - right_x
                dy = own_y[start : start + step, :] - right_y
                square = jnp.maximum(dx * dx + dy * dy, 1e-30)
                scaled = square * lax.rsqrt(square)
                parts.append(((1.0 + scaled) * jnp.exp2(scaled * to_two)).astype(BF16))
            halves.append(jnp.concatenate(parts, axis=0))
        tile = jnp.concatenate(halves, axis=1)
        left = jnp.concatenate([block[0:rhs, :], block[rhs : 2 * rhs, :]], axis=1)
        return acc + dot_bf16(left, tile, ((1,), (1,)))

    def some_blocks(index, acc):
        for inner in range(batch):
            acc = one_block(index * batch + inner, acc)
        return acc

    batch = math.gcd(blocks, 16)
    product = jnp.zeros((rhs, count), F32)
    if blocks == batch:
        product = some_blocks(0, product)
    else:
        product = lax.fori_loop(0, blocks // batch, some_blocks, product)

    edges = all_ref[:, 2 * rhs :, :].astype(F32).reshape(blocks * 8, LANES)
    place = lax.broadcasted_iota(jnp.int32, (blocks * 8, count), 0)
    kind = place % 8
    good = ((kind == 4) | (kind == 5)) & (place // 8 != skip)
    match = good & (edges[:, 3 * rhs : 3 * rhs + 1] == own[1:2, :])
    sums = dot_bf16(edges.astype(BF16), match.astype(F32).astype(BF16), ((0,), (0,)))
    extra = sums[0:rhs] + sums[rhs : 2 * rhs] + sums[2 * rhs : 3 * rhs]
    return product, extra, sums[3 * rhs + 1 : 3 * rhs + 2]


def first_kernel(where_ref, own_ref, res_ref, all_ref, product_ref, sums_ref, norm_ref, own_x, own_y):
    product, extra, number = half_product(where_ref[0], own_ref, all_ref, own_x, own_y)
    product_ref[...] = product
    sums_ref[0:32, :] = own_ref[0:32, :] + extra
    sums_ref[32:40, :] = own_ref[32:40, :]
    sums_ref[32:33, :] = own_ref[32:33, :] + number
    norm_ref[...] = dot_f32(res_ref[...], res_ref[...], ((1,), (1,)))


def second_kernel(
    whole_count, dir_ref, res_ref, norm_ref, product_ref, sums_ref, all_ref, image_ref, gram_ref, own_x, own_y
):
    product, extra, number = half_product(-1, sums_ref, all_ref, own_x, own_y)
    product = product + product_ref[...]
    size = sums_ref[32:33, :] + number
    district_part = (sums_ref[0:32, :] + extra) / jnp.sqrt(size)
    direction = dir_ref[...]
    kernel_scale = 1.0 / (corr_range * math.sqrt(whole_count))
    image = sums_ref[34:35, :] * direction + product * kernel_scale + district_gain * district_part
    image_ref[...] = image
    right = jnp.concatenate([direction, res_ref[...], image], axis=0)
    gram_ref[:, 0:96] = dot_f32(image, right, ((1,), (1,)))
    gram_ref[:, 96:128] = norm_ref[...]


def eliminate(work, step):
    rows = lax.broadcasted_iota(jnp.int32, work.shape, 0)
    one, two = work[:, step : step + 1], work[:, step + 1 : step + 2]
    one, two = jnp.broadcast_to(one, work.shape), jnp.broadcast_to(two, work.shape)
    row_one, row_two = work[step : step + 1, :], work[step + 1 : step + 2, :]
    p11, p12 = one[step : step + 1, :], two[step : step + 1, :]
    p21, p22 = one[step + 1 : step + 2, :], two[step + 1 : step + 2, :]
    inverse = 1.0 / (p11 * p22 - p12 * p21)
    new_one = (p22 * row_one - p12 * row_two) * inverse
    new_two = (p11 * row_two - p21 * row_one) * inverse
    rest = work - one * new_one - two * new_two
    return jnp.where(rows == step, new_one, jnp.where(rows == step + 1, new_two, rest))


def final_kernel(gram_ref, sol_ref, res_ref, dir_ref, image_ref, new_sol_ref, new_res_ref, new_dir_ref):
    rhs = 32
    total = gram_ref[0]
    for n in range(1, gram_ref.shape[0]):
        total = total + gram_ref[n]
    curv = total[:, 0:32]
    cross = total[:, 32:64]
    gram_image = total[:, 64:96]
    old_norm = total[:, 96:128]
    curv = 0.5 * (curv + curv.T)
    first = jnp.concatenate([curv, old_norm, cross, gram_image], axis=1)
    second = jnp.concatenate([old_norm, cross.T, jnp.zeros((rhs, 64), F32)], axis=1)
    for step in range(0, rhs, 2):
        first = eliminate(first, step)
        second = eliminate(second, step)
    alpha = first[:, 32:64]
    row = lax.broadcasted_iota(jnp.int32, (rhs, rhs), 0)
    col = lax.broadcasted_iota(jnp.int32, (rhs, rhs), 1)
    eye = (row == col).astype(F32)
    beta = eye - first[:, 64:96] + dot_f32(first[:, 96:128] - second[:, 32:64], alpha, ((1,), (0,)))
    direction = dir_ref[...]
    new_sol_ref[...] = sol_ref[...] + dot_f32(alpha, direction, ((0,), (0,)))
    new_res = res_ref[...] - dot_f32(alpha, image_ref[...], ((0,), (0,)))
    new_res_ref[...] = new_res
    new_dir_ref[...] = new_res + dot_f32(beta, direction, ((0,), (0,)))


VMEM_LIMIT = 48 * 1024 * 1024


def per_device(chips, points, noise_var, district, solution, residual, direction):
    rhs, count = direction.shape
    whole_count = count * chips * 2
    group = ("row", "pair")
    swap = [(0, 1), (1, 0)]
    params = pltpu.CompilerParams(vmem_limit_bytes=VMEM_LIMIT)
    wide = jax.ShapeDtypeStruct((rhs, count), F32)
    own_shape = jax.ShapeDtypeStruct((rhs + 8, count), F32)
    vmem = pl.BlockSpec(memory_space=pltpu.VMEM)
    block, own = pl.pallas_call(
        pack_kernel,
        out_shape=(jax.ShapeDtypeStruct((ROWS, LANES), BF16), own_shape),
        name="pack",
    )(points, district.reshape(1, count), noise_var.reshape(1, count), direction)
    near = lax.all_to_all(jnp.broadcast_to(block[None], (chips, ROWS, LANES)), group, 0, 0)
    far = lax.ppermute(near, "side", swap)
    where = lax.axis_index(group).astype(jnp.int32).reshape(1)
    own_scratch = [pltpu.VMEM((count, LANES), F32), pltpu.VMEM((count, LANES), F32)]
    product, sums, norm = pl.pallas_call(
        first_kernel,
        out_shape=(wide, own_shape, jax.ShapeDtypeStruct((rhs, rhs), F32)),
        in_specs=[pl.BlockSpec(memory_space=pltpu.SMEM)] + [vmem] * 3,
        out_specs=(vmem,) * 3,
        scratch_shapes=own_scratch,
        compiler_params=params,
        name="near_half",
    )(where, own, residual, near)
    image, gram = pl.pallas_call(
        functools.partial(second_kernel, whole_count),
        out_shape=(wide, jax.ShapeDtypeStruct((rhs, LANES), F32)),
        in_specs=[vmem] * 6,
        out_specs=(vmem, vmem),
        scratch_shapes=own_scratch,
        compiler_params=params,
        name="far_half",
    )(direction, residual, norm, product, sums, far)
    chip_gram = gram + lax.ppermute(gram, "side", swap)
    grams = lax.all_to_all(jnp.broadcast_to(chip_gram[None], (chips, rhs, LANES)), group, 0, 0)
    return pl.pallas_call(
        final_kernel,
        out_shape=(wide,) * 3,
        in_specs=[vmem] * 5,
        out_specs=(vmem,) * 3,
        compiler_params=params,
        name="final",
    )(grams, solution, residual, direction, image)


def solution(mesh):
    rows, cols = mesh.shape["row"], mesh.shape["col"]
    paired = Mesh(mesh.devices.reshape(rows, cols // 2, 2), ("row", "pair", "side"))
    samples = ("row", "pair", "side")
    wide, flat = P(None, samples), P(samples)
    return jax.shard_map(
        functools.partial(per_device, rows * cols // 2),
        mesh=paired,
        in_specs=(wide, flat, flat, wide, wide, wide),
        out_specs=(wide, wide, wide),
        check_vma=False,
    )
```

```python
import functools
import math

import jax
import jax.numpy as jnp
from jax import lax
from jax.experimental import pallas as pl
from jax.experimental.pallas import tpu as pltpu
from jax.sharding import Mesh, PartitionSpec as P

root_three = math.sqrt(3.0)
corr_range = 0.05
district_gain = 0.5
LANES = 128
ROWS = 72
F32, BF16 = jnp.float32, jnp.bfloat16


def dot_f32(left, right, dims):
    return lax.dot_general(
        left, right, (dims, ((), ())), precision=lax.Precision.HIGHEST, preferred_element_type=F32
    )


def dot_bf16(left, right, dims):
    return lax.dot_general(left, right, (dims, ((), ())), preferred_element_type=F32)


def three_pieces(vals):
    high = vals.astype(BF16)
    rest = vals - high.astype(F32)
    mid = rest.astype(BF16)
    low = (rest - mid.astype(F32)).astype(BF16)
    return high, mid, low


def stack_pieces(vals):
    rows, count = vals.shape
    ones = jnp.ones((LANES - 3 * rows, count), BF16)
    return jnp.concatenate([*three_pieces(vals), ones], axis=0)


def pack_kernel(
    points_hbm, dist_hbm, noise_hbm, dir_hbm, pack_ref, own_ref, points_ref, dist_ref, noise_ref, dir_ref, sems
):
    pairs = ((points_hbm, points_ref), (dist_hbm, dist_ref), (noise_hbm, noise_ref), (dir_hbm, dir_ref))
    copies = [pltpu.make_async_copy(src, dst, sems.at[n]) for n, (src, dst) in enumerate(pairs)]
    for copy in copies:
        copy.start()
    for copy in copies:
        copy.wait()
    rhs, count = dir_ref.shape
    dist = dist_ref[...]
    pts = points_ref[...].astype(F32)
    own_ref[...] = jnp.concatenate(
        [pts, dist.astype(F32), noise_ref[...], jnp.zeros((4, count), F32)], axis=0
    )
    stacked = stack_pieces(dir_ref[...])
    high = stacked[0:rhs]
    first = dist[:, 0:1]
    last = dist[:, count - 1 : count]
    row = lax.broadcasted_iota(jnp.int32, (8, count), 0)
    picked = jnp.where(row == 0, first, last)
    wanted = (row == 0) | ((row == 1) & (first != last))
    mask = (wanted & (dist == picked)).astype(F32).astype(BF16)
    edge = dot_bf16(mask, stacked, ((1,), (1,)))
    total = edge + pltpu.roll(edge, LANES - rhs, 1) + pltpu.roll(edge, LANES - 2 * rhs, 1)
    lane = lax.broadcasted_iota(jnp.int32, (8, LANES), 1)
    total = jnp.where(lane < rhs, total, 0.0)
    e_high, e_mid, e_low = three_pieces(total)
    row8 = lax.broadcasted_iota(jnp.int32, (8, LANES), 0)
    label = jnp.where(row8 == 0, first, last).astype(F32)
    extras = (
        e_high.astype(F32)
        + pltpu.roll(e_mid.astype(F32), rhs, 1)
        + pltpu.roll(e_low.astype(F32), 2 * rhs, 1)
    )
    extras = jnp.where(lane == 3 * rhs, label, extras)
    extras = jnp.where(lane == 3 * rhs + 1, edge, extras)
    tail = jnp.concatenate(
        [pts[:, 0:LANES], pts[:, LANES:], extras[0:2, :], jnp.zeros((2, LANES), F32)], axis=0
    )
    pack_ref[0:rhs, :] = high[:, 0:LANES]
    pack_ref[rhs : 2 * rhs, :] = high[:, LANES:]
    pack_ref[2 * rhs :, :] = tail.astype(BF16)


def own_side(own):
    scale = 3.0 / corr_range**2
    row = lax.broadcasted_iota(jnp.int32, own.shape, 0)
    cross = jnp.where(row < 2, own * (-2.0 * scale), 0.0)
    square = own * own
    norm = scale * (square[0:1] + square[1:2])
    cross_high, cross_low, _ = three_pieces(cross)
    high, mid, low = (piece.astype(F32) for piece in three_pieces(norm))
    ones = jnp.where(row < 2, scale, 0.0)
    norms = jnp.where(row == 0, high, jnp.where(row == 1, mid, jnp.where(row == 2, low, 0.0)))
    return jnp.concatenate([cross_high.astype(F32), cross_low.astype(F32), ones, ones, norms], axis=0)


def other_side(tail):
    left = tail.astype(F32)
    right = pltpu.roll(left, left.shape[0] - 2, 0)
    coords = jnp.concatenate([left, right], axis=1)
    square = coords * coords
    high = square.astype(BF16).astype(F32)
    return jnp.concatenate([coords, coords, high, square - high, jnp.ones_like(coords)], axis=0).astype(BF16)


def half_product(skip, own_ref, all_ref, side):
    blocks = all_ref.shape[0]
    count = own_ref.shape[1]
    rhs = 32
    own = own_ref[...]
    side[...] = own_side(own).T.astype(BF16)
    to_two = -math.log2(math.e)

    def one_block(index, acc):
        block = all_ref[index]
        square = dot_bf16(side[...], other_side(block[2 * rhs :, :]), ((1,), (0,)))
        square = jnp.maximum(square, 1e-30)
        scaled = square * lax.rsqrt(square)
        tile = ((1.0 + scaled) * jnp.exp2(scaled * to_two)).astype(BF16)
        left = jnp.concatenate([block[0:rhs, :], block[rhs : 2 * rhs, :]], axis=1)
        return acc + dot_bf16(left, tile, ((1,), (1,)))

    def some_blocks(index, acc):
        for inner in range(batch):
            acc = one_block(index * batch + inner, acc)
        return acc

    batch = math.gcd(blocks, 16)
    product = jnp.zeros((rhs, count), F32)
    if blocks == batch:
        product = some_blocks(0, product)
    else:
        product = lax.fori_loop(0, blocks // batch, some_blocks, product)

    edges = all_ref[:, 2 * rhs :, :].astype(F32).reshape(blocks * 8, LANES)
    place = lax.broadcasted_iota(jnp.int32, (blocks * 8, count), 0)
    kind = place % 8
    good = ((kind == 4) | (kind == 5)) & (place // 8 != skip)
    match = good & (edges[:, 3 * rhs : 3 * rhs + 1] == own[2:3, :])
    sums = dot_bf16(edges.astype(BF16), match.astype(F32).astype(BF16), ((0,), (0,)))
    extra = sums[0:rhs] + sums[rhs : 2 * rhs] + sums[2 * rhs : 3 * rhs]
    return product, extra, sums[3 * rhs + 1 : 3 * rhs + 2]


def first_kernel(own_ref, dir_ref, res_ref, all_ref, product_ref, sums_ref, norm_ref, side):
    rhs, count = dir_ref.shape
    product, extra, number = half_product(lax.axis_index(("row", "pair")), own_ref, all_ref, side)
    product_ref[...] = product
    labels = lax.broadcasted_iota(jnp.int32, (64, count), 0).astype(F32)
    onehot = (labels == own_ref[2:3, :]).astype(F32).astype(BF16)
    same = dot_bf16(onehot, onehot, ((0,), (0,))).astype(BF16)
    sums = dot_bf16(stack_pieces(dir_ref[...]), same, ((1,), (0,)))
    sums_ref[0:rhs, :] = sums[0:rhs] + sums[rhs : 2 * rhs] + sums[2 * rhs : 3 * rhs] + extra
    sums_ref[rhs:, :] = sums[3 * rhs : 3 * rhs + 8] + number
    norm_ref[...] = dot_f32(res_ref[...], res_ref[...], ((1,), (1,)))


def second_kernel(
    whole_count, own_ref, dir_ref, res_ref, norm_ref, product_ref, sums_ref, all_ref,
    image_ref, keep_ref, send_ref, side, gram,
):
    product, extra, number = half_product(-1, own_ref, all_ref, side)
    product = product + product_ref[...]
    size = sums_ref[32:33, :] + number
    district_part = (sums_ref[0:32, :] + extra) / jnp.sqrt(size)
    direction = dir_ref[...]
    kernel_scale = 1.0 / (corr_range * math.sqrt(whole_count))
    image = own_ref[3:4, :] * direction + product * kernel_scale + district_gain * district_part
    image_ref[...] = image
    right = jnp.concatenate([direction, res_ref[...], image], axis=0)
    gram[:, 0:96] = dot_f32(image, right, ((1,), (1,)))
    gram[:, 96:128] = norm_ref[...]
    half = keep_ref.shape[0]
    core = lax.axis_index("side")
    keep_ref[...] = gram[pl.ds(pl.multiple_of(core * half, half), half), :]
    send_ref[...] = gram[pl.ds(pl.multiple_of((1 - core) * half, half), half), :]


def eliminate(work, step):
    rows = lax.broadcasted_iota(jnp.int32, work.shape, 0)
    cols = [jnp.broadcast_to(work[:, step + n : step + n + 1], work.shape) for n in range(4)]
    line = [work[step + n : step + n + 1, :] for n in range(4)]
    piv = [[cols[m][step + n : step + n + 1, :] for m in range(4)] for n in range(4)]
    inverse = 1.0 / (piv[0][0] * piv[1][1] - piv[0][1] * piv[1][0])

    def first_block(top, bottom):
        return (piv[1][1] * top - piv[0][1] * bottom) * inverse, (piv[0][0] * bottom - piv[1][0] * top) * inverse

    new0, new1 = first_block(line[0], line[1])
    cross = [first_block(piv[0][m], piv[1][m]) for m in (2, 3)]
    rest = [[piv[n][m + 2] - piv[n][0] * cross[m][0] - piv[n][1] * cross[m][1] for m in range(2)] for n in (2, 3)]
    inverse_rest = 1.0 / (rest[0][0] * rest[1][1] - rest[0][1] * rest[1][0])
    left2 = line[2] - piv[2][0] * new0 - piv[2][1] * new1
    left3 = line[3] - piv[3][0] * new0 - piv[3][1] * new1
    new2 = (rest[1][1] * left2 - rest[0][1] * left3) * inverse_rest
    new3 = (rest[0][0] * left3 - rest[1][0] * left2) * inverse_rest
    new0 = new0 - cross[0][0] * new2 - cross[1][0] * new3
    new1 = new1 - cross[0][1] * new2 - cross[1][1] * new3
    work = work - (cols[0] * new0 + cols[1] * new1) - (cols[2] * new2 + cols[3] * new3)
    for n, new in enumerate((new0, new1, new2, new3)):
        work = jnp.where(rows == step + n, new, work)
    return work


def final_kernel(
    mine_ref, other_ref, sol_ref, res_ref, dir_ref, image_ref, new_sol_ref, new_res_ref, new_dir_ref, gram
):
    rhs = 32
    half = mine_ref.shape[0]
    core = lax.axis_index("side")
    gram[pl.ds(pl.multiple_of(core * half, half), half), :] = mine_ref[...]
    gram[pl.ds(pl.multiple_of((1 - core) * half, half), half), :] = other_ref[...]
    total = gram[...]
    curv = total[:, 0:32]
    cross = total[:, 32:64]
    gram_image = total[:, 64:96]
    old_norm = total[:, 96:128]
    curv = 0.5 * (curv + curv.T)
    first = jnp.concatenate([curv, old_norm, cross, gram_image], axis=1)
    second = jnp.concatenate([old_norm, cross.T, jnp.zeros((rhs, 64), F32)], axis=1)
    for step in range(0, rhs, 4):
        first = eliminate(first, step)
        second = eliminate(second, step)
    alpha = first[:, 32:64]
    row = lax.broadcasted_iota(jnp.int32, (rhs, rhs), 0)
    col = lax.broadcasted_iota(jnp.int32, (rhs, rhs), 1)
    eye = (row == col).astype(F32)
    beta = eye - first[:, 64:96] + dot_f32(first[:, 96:128] - second[:, 32:64], alpha, ((1,), (0,)))
    direction = dir_ref[...]
    new_sol_ref[...] = sol_ref[...] + dot_f32(alpha, direction, ((0,), (0,)))
    new_res = res_ref[...] - dot_f32(alpha, image_ref[...], ((0,), (0,)))
    new_res_ref[...] = new_res
    new_dir_ref[...] = new_res + dot_f32(beta, direction, ((0,), (0,)))


def call(kernel, outs, ins, name, megabytes, scratch=(), space=pltpu.VMEM):
    return pl.pallas_call(
        kernel,
        out_shape=tuple(jax.ShapeDtypeStruct(*out) for out in outs),
        in_specs=[pl.BlockSpec(memory_space=space)] * len(ins),
        out_specs=(pl.BlockSpec(memory_space=pltpu.VMEM),) * len(outs),
        scratch_shapes=scratch,
        compiler_params=pltpu.CompilerParams(vmem_limit_bytes=megabytes << 20),
        name=name,
    )(*ins)


def per_device(chips, points, noise_var, district, solution, residual, direction):
    rhs, count = direction.shape
    whole_count = count * chips * 2
    group = ("row", "pair")
    swap = [(0, 1), (1, 0)]
    wide = ((rhs, count), F32)
    half = ((rhs // 2, LANES), F32)
    side = pltpu.VMEM((count, 40), BF16)
    gram = pltpu.VMEM((rhs, LANES), F32)
    fetched = (points, district.reshape(1, count), noise_var.reshape(1, count), direction)
    block, own = call(
        pack_kernel,
        (((ROWS, LANES), BF16), ((8, count), F32)),
        fetched,
        "pack", 4,
        [pltpu.VMEM(arg.shape, arg.dtype) for arg in fetched] + [pltpu.SemaphoreType.DMA((len(fetched),))],
        pltpu.HBM,
    )
    near = lax.all_to_all(jnp.broadcast_to(block[None], (chips, ROWS, LANES)), group, 0, 0)
    far = lax.ppermute(near, "side", swap)
    product, sums, norm = call(
        first_kernel,
        (wide, ((rhs + 8, count), F32), ((rhs, rhs), F32)),
        (own, direction, residual, near),
        "near_half", 24, [side],
    )
    image, keep, send = call(
        functools.partial(second_kernel, whole_count),
        (wide, half, half),
        (own, direction, residual, norm, product, sums, far),
        "far_half", 24, [side, gram],
    )
    chip_half = keep + lax.ppermute(send, "side", swap)
    halves = lax.all_to_all(jnp.broadcast_to(chip_half[None], (chips, *half[0])), group, 0, 0)
    mine = jnp.sum(halves, axis=0)
    other = lax.ppermute(mine, "side", swap)
    return call(
        final_kernel,
        (wide,) * 3,
        (mine, other, solution, residual, direction, image),
        "final", 8, [gram],
    )


def solution(mesh):
    rows, cols = mesh.shape["row"], mesh.shape["col"]
    paired = Mesh(mesh.devices.reshape(rows, cols // 2, 2), ("row", "pair", "side"))
    samples = ("row", "pair", "side")
    wide, flat = P(None, samples), P(samples)
    return jax.shard_map(
        functools.partial(per_device, rows * cols // 2),
        mesh=paired,
        in_specs=(wide, flat, flat, wide, wide, wide),
        out_specs=(wide, wide, wide),
        check_vma=False,
    )
```

```python
import functools
import math

import jax
import jax.numpy as jnp
from jax import lax
from jax.experimental import pallas as pl
from jax.experimental.pallas import tpu as pltpu
from jax.sharding import Mesh, PartitionSpec as P

root_three = math.sqrt(3.0)
corr_range = 0.05
district_gain = 0.5
LANES = 128
ROWS = 72
F32, BF16 = jnp.float32, jnp.bfloat16


def dot_f32(left, right, dims):
    return lax.dot_general(
        left, right, (dims, ((), ())), precision=lax.Precision.HIGHEST, preferred_element_type=F32
    )


def dot_bf16(left, right, dims):
    return lax.dot_general(left, right, (dims, ((), ())), preferred_element_type=F32)


def three_pieces(vals):
    high = vals.astype(BF16)
    rest = vals - high.astype(F32)
    mid = rest.astype(BF16)
    low = (rest - mid.astype(F32)).astype(BF16)
    return high, mid, low


def stack_pieces(vals):
    rows, count = vals.shape
    ones = jnp.ones((LANES - 3 * rows, count), BF16)
    return jnp.concatenate([*three_pieces(vals), ones], axis=0)


def pack_kernel(
    points_hbm, dist_hbm, noise_hbm, dir_hbm, pack_ref, own_ref, points_ref, dist_ref, noise_ref, dir_ref, sems
):
    pairs = ((points_hbm, points_ref), (dist_hbm, dist_ref), (noise_hbm, noise_ref), (dir_hbm, dir_ref))
    copies = [pltpu.make_async_copy(src, dst, sems.at[n]) for n, (src, dst) in enumerate(pairs)]
    for copy in copies:
        copy.start()
    for copy in copies:
        copy.wait()
    rhs, count = dir_ref.shape
    dist = dist_ref[...]
    pts = points_ref[...].astype(F32)
    own_ref[...] = jnp.concatenate(
        [pts, dist.astype(F32), noise_ref[...], jnp.zeros((4, count), F32)], axis=0
    )
    high, mid, low = three_pieces(dir_ref[...])
    first = dist[:, 0:1]
    last = dist[:, count - 1 : count]
    row = lax.broadcasted_iota(jnp.int32, (8, count), 0)
    picked = jnp.where(row == 0, first, last)
    wanted = (row == 0) | ((row == 1) & (first != last))
    mask = (wanted & (dist == picked)).astype(F32).astype(BF16)
    ones = jnp.ones((LANES - 3 * rhs, count), BF16)
    edge = dot_bf16(mask, jnp.concatenate([high, high, high, ones], axis=0), ((1,), (1,)))
    edge = edge + dot_bf16(mask, jnp.concatenate([mid, mid, mid, 0 * ones], axis=0), ((1,), (1,)))
    edge = edge + dot_bf16(mask, jnp.concatenate([low, low, low, 0 * ones], axis=0), ((1,), (1,)))
    e_high, e_mid, e_low = (piece.astype(F32) for piece in three_pieces(edge))
    lane = lax.broadcasted_iota(jnp.int32, (8, LANES), 1)
    row8 = lax.broadcasted_iota(jnp.int32, (8, LANES), 0)
    label = jnp.where(row8 == 0, first, last).astype(F32)
    extras = jnp.where(lane < rhs, e_high, jnp.where(lane < 2 * rhs, e_mid, e_low))
    extras = jnp.where(lane == 3 * rhs, label, jnp.where(lane > 3 * rhs, edge, extras))
    tail = jnp.concatenate(
        [pts[:, 0:LANES], pts[:, LANES:], extras[0:2, :], jnp.zeros((2, LANES), F32)], axis=0
    )
    pack_ref[0:rhs, :] = high[:, 0:LANES]
    pack_ref[rhs : 2 * rhs, :] = high[:, LANES:]
    pack_ref[2 * rhs :, :] = tail.astype(BF16)


def own_side(own):
    scale = 3.0 / corr_range**2
    row = lax.broadcasted_iota(jnp.int32, own.shape, 0)
    cross = jnp.where(row < 2, own * (-2.0 * scale), 0.0)
    square = own * own
    norm = scale * (square[0:1] + square[1:2])
    cross_high, cross_low, _ = three_pieces(cross)
    high, mid, low = (piece.astype(F32) for piece in three_pieces(norm))
    ones = jnp.where(row < 2, scale, 0.0)
    norms = jnp.where(row == 0, high, jnp.where(row == 1, mid, jnp.where(row == 2, low, 0.0)))
    return jnp.concatenate([cross_high.astype(F32), cross_low.astype(F32), ones, ones, norms], axis=0)


def other_side(tail):
    left = tail.astype(F32)
    right = pltpu.roll(left, left.shape[0] - 2, 0)
    coords = jnp.concatenate([left, right], axis=1)
    square = coords * coords
    high = square.astype(BF16).astype(F32)
    return jnp.concatenate([coords, coords, high, square - high, jnp.ones_like(coords)], axis=0).astype(BF16)


def half_product(skip, own_ref, all_ref, side):
    blocks = all_ref.shape[0]
    count = own_ref.shape[1]
    rhs = 32
    to_two = -math.log2(math.e)

    def one_block(index, acc):
        block = all_ref[index]
        square = dot_bf16(side[...], other_side(block[2 * rhs :, :]), ((1,), (0,)))
        square = jnp.maximum(square, 1e-30)
        scaled = square * lax.rsqrt(square)
        tile = ((1.0 + scaled) * jnp.exp2(scaled * to_two)).astype(BF16)
        left = jnp.concatenate([block[0:rhs, :], block[rhs : 2 * rhs, :]], axis=1)
        return acc + dot_bf16(left, tile, ((1,), (1,)))

    def some_blocks(index, acc):
        for inner in range(batch):
            acc = one_block(index * batch + inner, acc)
        return acc

    batch = math.gcd(blocks, 16)
    product = jnp.zeros((rhs, count), F32)
    if blocks == batch:
        product = some_blocks(0, product)
    else:
        product = lax.fori_loop(0, blocks // batch, some_blocks, product)

    edges = all_ref[:, 2 * rhs :, :].astype(F32).reshape(blocks * 8, LANES)
    place = lax.broadcasted_iota(jnp.int32, (blocks * 8, count), 0)
    kind = place % 8
    good = ((kind == 4) | (kind == 5)) & (place // 8 != skip)
    match = good & (edges[:, 3 * rhs : 3 * rhs + 1] == own_ref[2:3, :])
    sums = dot_bf16(edges.astype(BF16), match.astype(F32).astype(BF16), ((0,), (0,)))
    extra = sums[0:rhs] + sums[rhs : 2 * rhs] + sums[2 * rhs : 3 * rhs]
    return product, extra, sums[3 * rhs + 1 : 3 * rhs + 2]


def first_kernel(own_ref, dir_ref, res_ref, all_ref, product_ref, sums_ref, norm_ref, side_ref):
    rhs, count = dir_ref.shape
    side_ref[...] = own_side(own_ref[...]).T.astype(BF16)
    product, extra, number = half_product(lax.axis_index(("row", "pair")), own_ref, all_ref, side_ref)
    product_ref[...] = product
    labels = lax.broadcasted_iota(jnp.int32, (64, count), 0).astype(F32)
    onehot = (labels == own_ref[2:3, :]).astype(F32).astype(BF16)
    same = dot_bf16(onehot, onehot, ((0,), (0,))).astype(BF16)
    sums = dot_bf16(stack_pieces(dir_ref[...]), same, ((1,), (0,)))
    sums_ref[0:rhs, :] = sums[0:rhs] + sums[rhs : 2 * rhs] + sums[2 * rhs : 3 * rhs] + extra
    sums_ref[rhs:, :] = sums[3 * rhs : 3 * rhs + 8] + number
    residual = res_ref[...]
    norm_ref[...] = jnp.zeros_like(norm_ref)
    norm_ref[:, 32:64] = dot_f32(residual, residual, ((1,), (1,)))


def second_kernel(
    whole_count, own_ref, dir_ref, res_ref, norm_ref, product_ref, sums_ref, side_ref, all_ref,
    image_ref, keep_ref, send_ref,
):
    product, extra, number = half_product(-1, own_ref, all_ref, side_ref)
    product = product + product_ref[...]
    size = sums_ref[32:33, :] + number
    district_part = (sums_ref[0:32, :] + extra) / jnp.sqrt(size)
    direction = dir_ref[...]
    kernel_scale = 1.0 / (corr_range * math.sqrt(whole_count))
    image = own_ref[3:4, :] * direction + product * kernel_scale + district_gain * district_part
    image_ref[...] = image
    part = 0.5 * direction
    none = jnp.zeros_like(part)
    gram = dot_f32(image, jnp.concatenate([part, none, res_ref[...], image], axis=0), ((1,), (1,)))
    gram = gram + dot_f32(part, jnp.concatenate([image, none, none, none], axis=0), ((1,), (1,)))
    gram = gram + norm_ref[...]
    half = keep_ref.shape[0]
    even = lax.axis_index("side") == 0
    keep_ref[...] = jnp.where(even, gram[:half], gram[half:])
    send_ref[...] = jnp.where(even, gram[half:], gram[:half])


def eliminate(work, step):
    rows = lax.broadcasted_iota(jnp.int32, work.shape, 0)
    cols = [jnp.broadcast_to(work[:, step + n : step + n + 1], work.shape) for n in range(4)]
    line = [work[step + n : step + n + 1, :] for n in range(4)]
    piv = [[cols[m][step + n : step + n + 1, :] for m in range(4)] for n in range(4)]
    inverse = 1.0 / (piv[0][0] * piv[1][1] - piv[0][1] * piv[1][0])

    def first_block(top, bottom):
        return (piv[1][1] * top - piv[0][1] * bottom) * inverse, (piv[0][0] * bottom - piv[1][0] * top) * inverse

    new0, new1 = first_block(line[0], line[1])
    cross = [first_block(piv[0][m], piv[1][m]) for m in (2, 3)]
    rest = [[piv[n][m + 2] - piv[n][0] * cross[m][0] - piv[n][1] * cross[m][1] for m in range(2)] for n in (2, 3)]
    inverse_rest = 1.0 / (rest[0][0] * rest[1][1] - rest[0][1] * rest[1][0])
    left2 = line[2] - piv[2][0] * new0 - piv[2][1] * new1
    left3 = line[3] - piv[3][0] * new0 - piv[3][1] * new1
    new2 = (rest[1][1] * left2 - rest[0][1] * left3) * inverse_rest
    new3 = (rest[0][0] * left3 - rest[1][0] * left2) * inverse_rest
    new0 = new0 - cross[0][0] * new2 - cross[1][0] * new3
    new1 = new1 - cross[0][1] * new2 - cross[1][1] * new3
    work = work - (cols[0] * new0 + cols[1] * new1) - (cols[2] * new2 + cols[3] * new3)
    for n, new in enumerate((new0, new1, new2, new3)):
        work = jnp.where(rows == step + n, new, work)
    return work


def final_kernel(mine_ref, other_ref, sol_ref, res_ref, dir_ref, image_ref, new_sol_ref, new_res_ref, new_dir_ref):
    rhs = sol_ref.shape[0]
    mine, other = mine_ref[...], other_ref[...]
    even = lax.axis_index("side") == 0
    first = jnp.concatenate([jnp.where(even, mine, other), jnp.where(even, other, mine)], axis=0)
    second = jnp.concatenate([first[:, 32:64], first[:, 64:96].T, jnp.zeros((rhs, 64), F32)], axis=1)
    for step in range(0, rhs, 4):
        first = eliminate(first, step)
        second = eliminate(second, step)
    alpha = first[:, 32:64]
    row = lax.broadcasted_iota(jnp.int32, (rhs, rhs), 0)
    col = lax.broadcasted_iota(jnp.int32, (rhs, rhs), 1)
    eye = (row == col).astype(F32)
    beta = eye - first[:, 64:96] + dot_f32(first[:, 96:128] - second[:, 32:64], alpha, ((1,), (0,)))
    direction = dir_ref[...]
    new_sol_ref[...] = sol_ref[...] + dot_f32(alpha, direction, ((0,), (0,)))
    new_res = res_ref[...] - dot_f32(alpha, image_ref[...], ((0,), (0,)))
    new_res_ref[...] = new_res
    new_dir_ref[...] = new_res + dot_f32(beta, direction, ((0,), (0,)))


def call(kernel, outs, ins, name, megabytes, scratch=(), space=pltpu.VMEM):
    return pl.pallas_call(
        kernel,
        out_shape=tuple(jax.ShapeDtypeStruct(*out) for out in outs),
        in_specs=[pl.BlockSpec(memory_space=space)] * len(ins),
        out_specs=(pl.BlockSpec(memory_space=pltpu.VMEM),) * len(outs),
        scratch_shapes=scratch,
        compiler_params=pltpu.CompilerParams(vmem_limit_bytes=megabytes << 20),
        name=name,
    )(*ins)


def per_device(chips, points, noise_var, district, solution, residual, direction):
    rhs, count = direction.shape
    whole_count = count * chips * 2
    group = ("row", "pair")
    swap = [(0, 1), (1, 0)]
    wide = ((rhs, count), F32)
    half = ((rhs // 2, LANES), F32)
    fetched = (points, district.reshape(1, count), noise_var.reshape(1, count), direction)
    fetched = tuple(pltpu.with_memory_space_constraint(arg, pltpu.HBM) for arg in fetched)
    block, own = call(
        pack_kernel,
        (((ROWS, LANES), BF16), ((8, count), F32)),
        fetched,
        "pack", 4,
        [pltpu.VMEM(arg.shape, arg.dtype) for arg in fetched] + [pltpu.SemaphoreType.DMA((len(fetched),))],
        pltpu.HBM,
    )
    near = lax.all_to_all(jnp.broadcast_to(block[None], (chips, ROWS, LANES)), group, 0, 0)
    far = lax.ppermute(near, "side", swap)
    product, sums, norm, side = call(
        first_kernel,
        (wide, ((rhs + 8, count), F32), ((rhs, LANES), F32), ((count, 40), BF16)),
        (own, direction, residual, near),
        "near_half", 24,
    )
    image, keep, send = call(
        functools.partial(second_kernel, whole_count),
        (wide, half, half),
        (own, direction, residual, norm, product, sums, side, far),
        "far_half", 24,
    )
    chip_half = keep + lax.ppermute(send, "side", swap)
    halves = lax.all_to_all(jnp.broadcast_to(chip_half[None], (chips, *half[0])), group, 0, 0)
    mine = jnp.sum(halves, axis=0)
    other = lax.ppermute(mine, "side", swap)
    return call(
        final_kernel,
        (wide,) * 3,
        (mine, other, solution, residual, direction, image),
        "final", 8,
    )


def solution(mesh):
    rows, cols = mesh.shape["row"], mesh.shape["col"]
    paired = Mesh(mesh.devices.reshape(rows, cols // 2, 2), ("row", "pair", "side"))
    samples = ("row", "pair", "side")
    wide, flat = P(None, samples), P(samples)
    return jax.shard_map(
        functools.partial(per_device, rows * cols // 2),
        mesh=paired,
        in_specs=(wide, flat, flat, wide, wide, wide),
        out_specs=(wide, wide, wide),
        check_vma=False,
    )
```

```python
import functools
import math

import jax
import jax.numpy as jnp
from jax import lax
from jax.experimental import pallas as pl
from jax.experimental.pallas import tpu as pltpu
from jax.sharding import Mesh, PartitionSpec as P

root_three = math.sqrt(3.0)
corr_range = 0.05
district_gain = 0.5
LANES = 128
ROWS = 72
F32, BF16 = jnp.float32, jnp.bfloat16


def dot_f32(left, right, dims):
    return lax.dot_general(
        left, right, (dims, ((), ())), precision=lax.Precision.HIGHEST, preferred_element_type=F32
    )


def dot_bf16(left, right, dims):
    return lax.dot_general(left, right, (dims, ((), ())), preferred_element_type=F32)


def three_pieces(vals):
    high = vals.astype(BF16)
    rest = vals - high.astype(F32)
    mid = rest.astype(BF16)
    low = (rest - mid.astype(F32)).astype(BF16)
    return high, mid, low


def stack_pieces(vals):
    rows, count = vals.shape
    ones = jnp.ones((LANES - 3 * rows, count), BF16)
    return jnp.concatenate([*three_pieces(vals), ones], axis=0)


def pack_kernel(
    points_hbm, dist_hbm, noise_hbm, dir_hbm, pack_ref, own_ref, points_ref, dist_ref, noise_ref, dir_ref, sems
):
    pairs = ((points_hbm, points_ref), (dist_hbm, dist_ref), (noise_hbm, noise_ref), (dir_hbm, dir_ref))
    copies = [pltpu.make_async_copy(src, dst, sems.at[n]) for n, (src, dst) in enumerate(pairs)]
    for copy in copies:
        copy.start()
    for copy in copies:
        copy.wait()
    rhs, count = dir_ref.shape
    dist = dist_ref[...]
    pts = points_ref[...].astype(F32)
    own_ref[...] = jnp.concatenate(
        [pts, dist.astype(F32), noise_ref[...], jnp.zeros((4, count), F32)], axis=0
    )
    high, mid, low = three_pieces(dir_ref[...])
    first = dist[:, 0:1]
    last = dist[:, count - 1 : count]
    row = lax.broadcasted_iota(jnp.int32, (8, count), 0)
    picked = jnp.where(row == 0, first, last)
    wanted = (row == 0) | ((row == 1) & (first != last))
    mask = (wanted & (dist == picked)).astype(F32).astype(BF16)
    ones = jnp.ones((LANES - 3 * rhs, count), BF16)
    edge = dot_bf16(mask, jnp.concatenate([high, high, high, ones], axis=0), ((1,), (1,)))
    edge = edge + dot_bf16(mask, jnp.concatenate([mid, mid, mid, 0 * ones], axis=0), ((1,), (1,)))
    edge = edge + dot_bf16(mask, jnp.concatenate([low, low, low, 0 * ones], axis=0), ((1,), (1,)))
    e_high, e_mid, e_low = (piece.astype(F32) for piece in three_pieces(edge))
    lane = lax.broadcasted_iota(jnp.int32, (8, LANES), 1)
    row8 = lax.broadcasted_iota(jnp.int32, (8, LANES), 0)
    label = jnp.where(row8 == 0, first, last).astype(F32)
    extras = jnp.where(lane < rhs, e_high, jnp.where(lane < 2 * rhs, e_mid, e_low))
    extras = jnp.where(lane == 3 * rhs, label, jnp.where(lane > 3 * rhs, edge, extras))
    tail = jnp.concatenate(
        [pts[:, 0:LANES], pts[:, LANES:], extras[0:2, :], jnp.zeros((2, LANES), F32)], axis=0
    )
    pack_ref[0:rhs, :] = high[:, 0:LANES]
    pack_ref[rhs : 2 * rhs, :] = high[:, LANES:]
    pack_ref[2 * rhs :, :] = tail.astype(BF16)


def own_side(own):
    scale = 3.0 / corr_range**2
    row = lax.broadcasted_iota(jnp.int32, own.shape, 0)
    cross = jnp.where(row < 2, own * (-2.0 * scale), 0.0)
    square = own * own
    norm = scale * (square[0:1] + square[1:2])
    cross_high, cross_low, _ = three_pieces(cross)
    high, mid, low = (piece.astype(F32) for piece in three_pieces(norm))
    ones = jnp.where(row < 2, scale, 0.0)
    norms = jnp.where(row == 0, high, jnp.where(row == 1, mid, jnp.where(row == 2, low, 0.0)))
    return jnp.concatenate([cross_high.astype(F32), cross_low.astype(F32), ones, ones, norms], axis=0)


def other_side(tail):
    left = tail.astype(F32)
    right = pltpu.roll(left, left.shape[0] - 2, 0)
    coords = jnp.concatenate([left, right], axis=1)
    square = coords * coords
    high = square.astype(BF16).astype(F32)
    return jnp.concatenate([coords, coords, high, square - high, jnp.ones_like(coords)], axis=0).astype(BF16)


def half_product(skip, own_ref, all_ref, side):
    blocks = all_ref.shape[0]
    count = own_ref.shape[1]
    rhs = 32
    to_two = -math.log2(math.e)

    def one_block(index, acc):
        block = all_ref[index]
        square = dot_bf16(side[...], other_side(block[2 * rhs :, :]), ((1,), (0,)))
        square = jnp.maximum(square, 1e-30)
        scaled = square * lax.rsqrt(square)
        tile = ((1.0 + scaled) * jnp.exp2(scaled * to_two)).astype(BF16)
        left = jnp.concatenate([block[0:rhs, :], block[rhs : 2 * rhs, :]], axis=1)
        return acc + dot_bf16(left, tile, ((1,), (1,)))

    def some_blocks(index, acc):
        for inner in range(batch):
            acc = one_block(index * batch + inner, acc)
        return acc

    batch = math.gcd(blocks, 16)
    product = jnp.zeros((rhs, count), F32)
    if blocks == batch:
        product = some_blocks(0, product)
    else:
        product = lax.fori_loop(0, blocks // batch, some_blocks, product)

    edges = all_ref[:, 2 * rhs :, :].astype(F32).reshape(blocks * 8, LANES)
    place = lax.broadcasted_iota(jnp.int32, (blocks * 8, count), 0)
    kind = place % 8
    good = ((kind == 4) | (kind == 5)) & (place // 8 != skip)
    match = good & (edges[:, 3 * rhs : 3 * rhs + 1] == own_ref[2:3, :])
    sums = dot_bf16(edges.astype(BF16), match.astype(F32).astype(BF16), ((0,), (0,)))
    extra = sums[0:rhs] + sums[rhs : 2 * rhs] + sums[2 * rhs : 3 * rhs]
    return product, extra, sums[3 * rhs + 1 : 3 * rhs + 2]


def first_kernel(own_ref, dir_ref, res_ref, all_ref, product_ref, sums_ref, norm_ref, side_ref):
    rhs, count = dir_ref.shape
    side_ref[...] = own_side(own_ref[...]).T.astype(BF16)
    product, extra, number = half_product(lax.axis_index(("row", "pair")), own_ref, all_ref, side_ref)
    product_ref[...] = product
    labels = lax.broadcasted_iota(jnp.int32, (64, count), 0).astype(F32)
    onehot = (labels == own_ref[2:3, :]).astype(F32).astype(BF16)
    same = dot_bf16(onehot, onehot, ((0,), (0,))).astype(BF16)
    sums = dot_bf16(stack_pieces(dir_ref[...]), same, ((1,), (0,)))
    sums_ref[0:rhs, :] = sums[0:rhs] + sums[rhs : 2 * rhs] + sums[2 * rhs : 3 * rhs] + extra
    sums_ref[rhs:, :] = sums[3 * rhs : 3 * rhs + 8] + number
    residual = res_ref[...]
    norm_ref[...] = jnp.zeros_like(norm_ref)
    norm_ref[:, 32:64] = dot_f32(residual, residual, ((1,), (1,)))


def second_kernel(
    whole_count, own_ref, dir_ref, res_ref, norm_ref, product_ref, sums_ref, side_ref, all_ref,
    image_ref, packed_ref,
):
    product, extra, number = half_product(-1, own_ref, all_ref, side_ref)
    product = product + product_ref[...]
    size = sums_ref[32:33, :] + number
    district_part = (sums_ref[0:32, :] + extra) / jnp.sqrt(size)
    direction = dir_ref[...]
    kernel_scale = 1.0 / (corr_range * math.sqrt(whole_count))
    image = own_ref[3:4, :] * direction + product * kernel_scale + district_gain * district_part
    image_ref[...] = image
    part = 0.5 * direction
    none = jnp.zeros_like(part)
    gram = dot_f32(image, jnp.concatenate([part, none, res_ref[...], image], axis=0), ((1,), (1,)))
    gram = gram + dot_f32(part, jnp.concatenate([image, none, none, none], axis=0), ((1,), (1,)))
    gram = gram + norm_ref[...]
    packed = pack_gram(gram)
    for n in range(6):
        packed_ref[n] = packed[n // 2][4 * (n % 2) : 4 * (n % 2) + 4, :]


def lane_groups(height):
    row = lax.broadcasted_iota(jnp.int32, (height, LANES), 0)
    lane = lax.broadcasted_iota(jnp.int32, (height, LANES), 1)
    return row, lane % 32, lane // 32


def pack_gram(gram):
    row, col, group = lane_groups(32)
    below = (col <= row) & (group <= 1)
    kept = jnp.where(below | (group == 2) | ((group == 3) & (col > row)), gram, 0.0)
    diag = jnp.sum(jnp.where((group == 3) & (col == row), gram, 0.0), axis=0, keepdims=True)
    diag = jnp.broadcast_to(diag, (8, LANES))
    row8, col8, group8 = lane_groups(8)
    packed = [jnp.zeros((8, LANES), F32)] * 3
    for n in range(4):
        rows = kept[8 * n : 8 * n + 8]
        for source, target in ((0, 1), (1, 2), (2, 0), (3, 1)):
            turn = (n - source) % 4 * 32
            moved = pltpu.roll(rows, turn, 1) if turn else rows
            packed[target] = packed[target] + jnp.where(group8 == n, moved, 0.0)
    packed[2] = packed[2] + jnp.where((group8 == 0) & (row8 == 0) & (col8 > 0), pltpu.roll(diag, 32, 1), 0.0)
    packed[2] = packed[2] + jnp.where((group8 == 0) & (row8 == 1) & (col8 == 2), pltpu.roll(diag, 34, 1), 0.0)
    return packed


def unpack_gram(packed):
    _, _, group8 = lane_groups(8)
    parts = []
    for n in range(4):
        rows = jnp.zeros((8, LANES), F32)
        for source, target in ((0, 1), (1, 2), (2, 0), (3, 1)):
            turn = (source - n) % 4 * 32
            moved = pltpu.roll(packed[target], turn, 1) if turn else packed[target]
            rows = jnp.where(group8 == source, moved, rows)
        parts.append(rows)
    flat = jnp.concatenate(parts, axis=0)
    turned = flat.T
    turned = jnp.concatenate([turned[0:32], turned[32:64], turned[64:96], turned[96:128]], axis=1)
    row, col, group = lane_groups(32)
    diag = jnp.where(col[0:1] == 0, pltpu.roll(flat[0:8], 62, 1)[1:2], pltpu.roll(flat[0:8], 64, 1)[0:1])
    direct = (group == 2) | ((group <= 1) & (col <= row)) | ((group == 3) & (col > row))
    first = jnp.where(direct, flat, jnp.where((group == 3) & (col == row), diag, turned))
    second = pltpu.roll(jnp.where(group == 1, first, turned), 96, 1)
    return first, second


def eliminate(work, step):
    rows = lax.broadcasted_iota(jnp.int32, work.shape, 0)
    cols = [jnp.broadcast_to(work[:, step + n : step + n + 1], work.shape) for n in range(4)]
    line = [work[step + n : step + n + 1, :] for n in range(4)]
    piv = [[cols[m][step + n : step + n + 1, :] for m in range(4)] for n in range(4)]
    inverse = 1.0 / (piv[0][0] * piv[1][1] - piv[0][1] * piv[1][0])

    def first_block(top, bottom):
        return (piv[1][1] * top - piv[0][1] * bottom) * inverse, (piv[0][0] * bottom - piv[1][0] * top) * inverse

    new0, new1 = first_block(line[0], line[1])
    cross = [first_block(piv[0][m], piv[1][m]) for m in (2, 3)]
    rest = [[piv[n][m + 2] - piv[n][0] * cross[m][0] - piv[n][1] * cross[m][1] for m in range(2)] for n in (2, 3)]
    inverse_rest = 1.0 / (rest[0][0] * rest[1][1] - rest[0][1] * rest[1][0])
    left2 = line[2] - piv[2][0] * new0 - piv[2][1] * new1
    left3 = line[3] - piv[3][0] * new0 - piv[3][1] * new1
    new2 = (rest[1][1] * left2 - rest[0][1] * left3) * inverse_rest
    new3 = (rest[0][0] * left3 - rest[1][0] * left2) * inverse_rest
    new0 = new0 - cross[0][0] * new2 - cross[1][0] * new3
    new1 = new1 - cross[0][1] * new2 - cross[1][1] * new3
    work = work - (cols[0] * new0 + cols[1] * new1) - (cols[2] * new2 + cols[3] * new3)
    for n, new in enumerate((new0, new1, new2, new3)):
        work = jnp.where(rows == step + n, new, work)
    return work


def final_kernel(mine_ref, other_ref, sol_ref, res_ref, dir_ref, image_ref, new_sol_ref, new_res_ref, new_dir_ref):
    rhs = sol_ref.shape[0]
    even = lax.axis_index("side") == 0
    quarters = [jnp.where(even, mine_ref[n], other_ref[n]) for n in range(3)]
    quarters += [jnp.where(even, other_ref[n], mine_ref[n]) for n in range(3)]
    first, second = unpack_gram([jnp.concatenate(quarters[2 * n : 2 * n + 2], axis=0) for n in range(3)])
    for step in range(0, rhs, 4):
        first = eliminate(first, step)
        second = eliminate(second, step)
    alpha = first[:, 32:64]
    row = lax.broadcasted_iota(jnp.int32, (rhs, rhs), 0)
    col = lax.broadcasted_iota(jnp.int32, (rhs, rhs), 1)
    eye = (row == col).astype(F32)
    beta = eye - first[:, 64:96] + dot_f32(first[:, 96:128] - second[:, 32:64], alpha, ((1,), (0,)))
    direction = dir_ref[...]
    new_sol_ref[...] = sol_ref[...] + dot_f32(alpha, direction, ((0,), (0,)))
    new_res = res_ref[...] - dot_f32(alpha, image_ref[...], ((0,), (0,)))
    new_res_ref[...] = new_res
    new_dir_ref[...] = new_res + dot_f32(beta, direction, ((0,), (0,)))


def call(kernel, outs, ins, name, megabytes, scratch=(), space=pltpu.VMEM):
    return pl.pallas_call(
        kernel,
        out_shape=tuple(jax.ShapeDtypeStruct(*out) for out in outs),
        in_specs=[pl.BlockSpec(memory_space=space)] * len(ins),
        out_specs=(pl.BlockSpec(memory_space=pltpu.VMEM),) * len(outs),
        scratch_shapes=scratch,
        compiler_params=pltpu.CompilerParams(vmem_limit_bytes=megabytes << 20),
        name=name,
    )(*ins)


def per_device(chips, points, noise_var, district, solution, residual, direction):
    rhs, count = direction.shape
    whole_count = count * chips * 2
    group = ("row", "pair")
    swap = [(0, 1), (1, 0)]
    wide = ((rhs, count), F32)
    fetched = (points, district.reshape(1, count), noise_var.reshape(1, count), direction)
    fetched = tuple(pltpu.with_memory_space_constraint(arg, pltpu.HBM) for arg in fetched)
    block, own = call(
        pack_kernel,
        (((ROWS, LANES), BF16), ((8, count), F32)),
        fetched,
        "pack", 4,
        [pltpu.VMEM(arg.shape, arg.dtype) for arg in fetched] + [pltpu.SemaphoreType.DMA((len(fetched),))],
        pltpu.HBM,
    )
    near = lax.all_to_all(jnp.broadcast_to(block[None], (chips, ROWS, LANES)), group, 0, 0)
    far = lax.ppermute(near, "side", swap)
    product, sums, norm, side = call(
        first_kernel,
        (wide, ((rhs + 8, count), F32), ((rhs, LANES), F32), ((count, 40), BF16)),
        (own, direction, residual, near),
        "near_half", 24,
    )
    image, packed = call(
        functools.partial(second_kernel, whole_count),
        (wide, ((6, 4, LANES), F32)),
        (own, direction, residual, norm, product, sums, side, far),
        "far_half", 24,
    )
    copies = jnp.broadcast_to(packed.reshape(1, 2, 3, 4, LANES), (chips, 2, 3, 4, LANES)).reshape(-1, 3, 4, LANES)
    mine = jnp.sum(lax.all_to_all(copies, group + ("side",), 0, 0, tiled=True), axis=0)
    other = lax.ppermute(mine, "side", swap)
    return call(
        final_kernel,
        (wide,) * 3,
        (mine, other, solution, residual, direction, image),
        "final", 8,
    )


def solution(mesh):
    rows, cols = mesh.shape["row"], mesh.shape["col"]
    paired = Mesh(mesh.devices.reshape(rows, cols // 2, 2), ("row", "pair", "side"))
    samples = ("row", "pair", "side")
    wide, flat = P(None, samples), P(samples)
    return jax.shard_map(
        functools.partial(per_device, rows * cols // 2),
        mesh=paired,
        in_specs=(wide, flat, flat, wide, wide, wide),
        out_specs=(wide, wide, wide),
        check_vma=False,
    )
```

```python
import functools
import math

import jax
import jax.numpy as jnp
from jax import lax
from jax.experimental import pallas as pl
from jax.experimental.pallas import tpu as pltpu
from jax.sharding import Mesh, PartitionSpec as P

root_three = math.sqrt(3.0)
corr_range = 0.05
district_gain = 0.5
LANES = 128
ROWS = 72
F32, BF16 = jnp.float32, jnp.bfloat16


def dot_f32(left, right, dims):
    return lax.dot_general(
        left, right, (dims, ((), ())), precision=lax.Precision.HIGHEST, preferred_element_type=F32
    )


def dot_bf16(left, right, dims):
    return lax.dot_general(left, right, (dims, ((), ())), preferred_element_type=F32)


def three_pieces(vals):
    high = vals.astype(BF16)
    rest = vals - high.astype(F32)
    mid = rest.astype(BF16)
    low = (rest - mid.astype(F32)).astype(BF16)
    return high, mid, low


def stack_pieces(vals):
    rows, count = vals.shape
    ones = jnp.ones((LANES - 3 * rows, count), BF16)
    return jnp.concatenate([*three_pieces(vals), ones], axis=0)


def pack_kernel(
    points_hbm, dist_hbm, noise_hbm, dir_hbm, pack_ref, own_ref, points_ref, dist_ref, noise_ref, dir_ref, sems
):
    pairs = ((points_hbm, points_ref), (dist_hbm, dist_ref), (noise_hbm, noise_ref), (dir_hbm, dir_ref))
    copies = [pltpu.make_async_copy(src, dst, sems.at[n]) for n, (src, dst) in enumerate(pairs)]
    for copy in copies:
        copy.start()
    for copy in copies:
        copy.wait()
    rhs, count = dir_ref.shape
    dist = dist_ref[...]
    pts = points_ref[...].astype(F32)
    own_ref[...] = jnp.concatenate(
        [pts, dist.astype(F32), noise_ref[...], jnp.zeros((4, count), F32)], axis=0
    )
    high, mid, low = three_pieces(dir_ref[...])
    first = dist[:, 0:1]
    last = dist[:, count - 1 : count]
    row = lax.broadcasted_iota(jnp.int32, (8, count), 0)
    picked = jnp.where(row == 0, first, last)
    wanted = (row == 0) | ((row == 1) & (first != last))
    mask = (wanted & (dist == picked)).astype(F32).astype(BF16)
    ones = jnp.ones((LANES - 3 * rhs, count), BF16)
    edge = dot_bf16(mask, jnp.concatenate([high, high, high, ones], axis=0), ((1,), (1,)))
    edge = edge + dot_bf16(mask, jnp.concatenate([mid, mid, mid, 0 * ones], axis=0), ((1,), (1,)))
    edge = edge + dot_bf16(mask, jnp.concatenate([low, low, low, 0 * ones], axis=0), ((1,), (1,)))
    e_high, e_mid, e_low = (piece.astype(F32) for piece in three_pieces(edge))
    lane = lax.broadcasted_iota(jnp.int32, (8, LANES), 1)
    row8 = lax.broadcasted_iota(jnp.int32, (8, LANES), 0)
    label = jnp.where(row8 == 0, first, last).astype(F32)
    extras = jnp.where(lane < rhs, e_high, jnp.where(lane < 2 * rhs, e_mid, e_low))
    extras = jnp.where(lane == 3 * rhs, label, jnp.where(lane > 3 * rhs, edge, extras))
    tail = jnp.concatenate(
        [pts[:, 0:LANES], pts[:, LANES:], extras[0:2, :], jnp.zeros((2, LANES), F32)], axis=0
    )
    pack_ref[0:rhs, :] = high[:, 0:LANES]
    pack_ref[rhs : 2 * rhs, :] = high[:, LANES:]
    pack_ref[2 * rhs :, :] = tail.astype(BF16)


def own_side(own):
    scale = 3.0 / corr_range**2
    row = lax.broadcasted_iota(jnp.int32, own.shape, 0)
    cross = jnp.where(row < 2, own * (-2.0 * scale), 0.0)
    square = own * own
    norm = scale * (square[0:1] + square[1:2])
    cross_high, cross_low, _ = three_pieces(cross)
    high, mid, low = (piece.astype(F32) for piece in three_pieces(norm))
    ones = jnp.where(row < 2, scale, 0.0)
    norms = jnp.where(row == 0, high, jnp.where(row == 1, mid, jnp.where(row == 2, low, 0.0)))
    return jnp.concatenate([cross_high.astype(F32), cross_low.astype(F32), ones, ones, norms], axis=0)


def other_side(tail):
    left = tail.astype(F32)
    right = pltpu.roll(left, left.shape[0] - 2, 0)
    coords = jnp.concatenate([left, right], axis=1)
    square = coords * coords
    high = square.astype(BF16).astype(F32)
    return jnp.concatenate([coords, coords, high, square - high, jnp.ones_like(coords)], axis=0).astype(BF16)


def half_product(skip, own_ref, all_ref, side):
    blocks = all_ref.shape[0]
    count = own_ref.shape[1]
    rhs = 32
    to_two = -math.log2(math.e)

    def one_block(index, acc):
        block = all_ref[index]
        square = dot_bf16(side[...], other_side(block[2 * rhs :, :]), ((1,), (0,)))
        square = jnp.maximum(square, 1e-30)
        scaled = square * lax.rsqrt(square)
        tile = ((1.0 + scaled) * jnp.exp2(scaled * to_two)).astype(BF16)
        left = jnp.concatenate([block[0:rhs, :], block[rhs : 2 * rhs, :]], axis=1)
        return acc + dot_bf16(left, tile, ((1,), (1,)))

    def some_blocks(index, acc):
        for inner in range(batch):
            acc = one_block(index * batch + inner, acc)
        return acc

    batch = math.gcd(blocks, 16)
    product = jnp.zeros((rhs, count), F32)
    if blocks == batch:
        product = some_blocks(0, product)
    else:
        product = lax.fori_loop(0, blocks // batch, some_blocks, product)

    edges = all_ref[:, 2 * rhs :, :].astype(F32).reshape(blocks * 8, LANES)
    place = lax.broadcasted_iota(jnp.int32, (blocks * 8, count), 0)
    kind = place % 8
    good = ((kind == 4) | (kind == 5)) & (place // 8 != skip)
    match = good & (edges[:, 3 * rhs : 3 * rhs + 1] == own_ref[2:3, :])
    sums = dot_bf16(edges.astype(BF16), match.astype(F32).astype(BF16), ((0,), (0,)))
    extra = sums[0:rhs] + sums[rhs : 2 * rhs] + sums[2 * rhs : 3 * rhs]
    return product, extra, sums[3 * rhs + 1 : 3 * rhs + 2]


def first_kernel(own_ref, dir_ref, res_ref, all_ref, product_ref, sums_ref, norm_ref, side_ref):
    rhs, count = dir_ref.shape
    side_ref[...] = own_side(own_ref[...]).T.astype(BF16)
    product, extra, number = half_product(lax.axis_index(("row", "pair")), own_ref, all_ref, side_ref)
    product_ref[...] = product
    labels = lax.broadcasted_iota(jnp.int32, (64, count), 0).astype(F32)
    onehot = (labels == own_ref[2:3, :]).astype(F32).astype(BF16)
    same = dot_bf16(onehot, onehot, ((0,), (0,))).astype(BF16)
    sums = dot_bf16(stack_pieces(dir_ref[...]), same, ((1,), (0,)))
    sums_ref[0:rhs, :] = sums[0:rhs] + sums[rhs : 2 * rhs] + sums[2 * rhs : 3 * rhs] + extra
    sums_ref[rhs:, :] = sums[3 * rhs : 3 * rhs + 8] + number
    residual = res_ref[...]
    norm_ref[...] = jnp.zeros_like(norm_ref)
    norm_ref[:, 32:64] = dot_f32(residual, residual, ((1,), (1,)))


def second_kernel(
    whole_count, own_ref, dir_ref, res_ref, norm_ref, product_ref, sums_ref, side_ref, all_ref,
    image_ref, packed_ref,
):
    product, extra, number = half_product(-1, own_ref, all_ref, side_ref)
    product = product + product_ref[...]
    size = sums_ref[32:33, :] + number
    district_part = (sums_ref[0:32, :] + extra) / jnp.sqrt(size)
    direction = dir_ref[...]
    kernel_scale = 1.0 / (corr_range * math.sqrt(whole_count))
    image = own_ref[3:4, :] * direction + product * kernel_scale + district_gain * district_part
    image_ref[...] = image
    part = 0.5 * direction
    none = jnp.zeros_like(part)
    gram = dot_f32(image, jnp.concatenate([part, none, res_ref[...], image], axis=0), ((1,), (1,)))
    gram = gram + dot_f32(part, jnp.concatenate([image, none, none, none], axis=0), ((1,), (1,)))
    gram = gram + norm_ref[...]
    packed = pack_gram(gram)
    for n in range(6):
        packed_ref[n] = packed[n // 2][4 * (n % 2) : 4 * (n % 2) + 4, :]


def lane_groups(height):
    row = lax.broadcasted_iota(jnp.int32, (height, LANES), 0)
    lane = lax.broadcasted_iota(jnp.int32, (height, LANES), 1)
    return row, lane % 32, lane // 32


def pack_gram(gram):
    row, col, group = lane_groups(32)
    below = (col <= row) & (group <= 1)
    kept = jnp.where(below | (group == 2) | ((group == 3) & (col > row)), gram, 0.0)
    diag = jnp.sum(jnp.where((group == 3) & (col == row), gram, 0.0), axis=0, keepdims=True)
    diag = jnp.broadcast_to(diag, (8, LANES))
    row8, col8, group8 = lane_groups(8)
    packed = [jnp.zeros((8, LANES), F32)] * 3
    for n in range(4):
        rows = kept[8 * n : 8 * n + 8]
        for source, target in ((0, 1), (1, 2), (2, 0), (3, 1)):
            turn = (n - source) % 4 * 32
            moved = pltpu.roll(rows, turn, 1) if turn else rows
            packed[target] = packed[target] + jnp.where(group8 == n, moved, 0.0)
    packed[2] = packed[2] + jnp.where((group8 == 0) & (row8 == 0) & (col8 > 0), pltpu.roll(diag, 32, 1), 0.0)
    packed[2] = packed[2] + jnp.where((group8 == 0) & (row8 == 1) & (col8 == 2), pltpu.roll(diag, 34, 1), 0.0)
    return packed


def unpack_gram(packed):
    _, _, group8 = lane_groups(8)
    parts = []
    for n in range(4):
        rows = jnp.zeros((8, LANES), F32)
        for source, target in ((0, 1), (1, 2), (2, 0), (3, 1)):
            turn = (source - n) % 4 * 32
            moved = pltpu.roll(packed[target], turn, 1) if turn else packed[target]
            rows = jnp.where(group8 == source, moved, rows)
        parts.append(rows)
    flat = jnp.concatenate(parts, axis=0)
    turned = flat.T
    turned = jnp.concatenate([turned[0:32], turned[32:64], turned[64:96], turned[96:128]], axis=1)
    row, col, group = lane_groups(32)
    diag = jnp.where(col[0:1] == 0, pltpu.roll(flat[0:8], 62, 1)[1:2], pltpu.roll(flat[0:8], 64, 1)[0:1])
    direct = (group == 2) | ((group <= 1) & (col <= row)) | ((group == 3) & (col > row))
    first = jnp.where(direct, flat, jnp.where((group == 3) & (col == row), diag, turned))
    second = pltpu.roll(jnp.where(group == 1, first, turned), 96, 1)
    return first, second


def solve_pair(a, b, c, d):
    inverse = 1.0 / a
    lower = c * inverse
    inverse_rest = 1.0 / (d - lower * b)

    def solve(top, bottom):
        second = (bottom - lower * top) * inverse_rest
        return (top - b * second) * inverse, second

    return solve


def eliminate(work, step):
    rows = lax.broadcasted_iota(jnp.int32, work.shape, 0)
    cols = [jnp.broadcast_to(work[:, step + n : step + n + 1], work.shape) for n in range(4)]
    line = [work[step + n : step + n + 1, :] for n in range(4)]
    piv = [[cols[m][step + n : step + n + 1, :] for m in range(4)] for n in range(4)]
    first_block = solve_pair(piv[0][0], piv[0][1], piv[1][0], piv[1][1])
    new0, new1 = first_block(line[0], line[1])
    cross = [first_block(piv[0][m], piv[1][m]) for m in (2, 3)]
    rest = [[piv[n][m + 2] - piv[n][0] * cross[m][0] - piv[n][1] * cross[m][1] for m in range(2)] for n in (2, 3)]
    left2 = line[2] - piv[2][0] * new0 - piv[2][1] * new1
    left3 = line[3] - piv[3][0] * new0 - piv[3][1] * new1
    new2, new3 = solve_pair(rest[0][0], rest[0][1], rest[1][0], rest[1][1])(left2, left3)
    new0 = new0 - cross[0][0] * new2 - cross[1][0] * new3
    new1 = new1 - cross[0][1] * new2 - cross[1][1] * new3
    work = work - (cols[0] * new0 + cols[1] * new1) - (cols[2] * new2 + cols[3] * new3)
    for n, new in enumerate((new0, new1, new2, new3)):
        work = jnp.where(rows == step + n, new, work)
    return work


def final_kernel(mine_ref, other_ref, sol_ref, res_ref, dir_ref, image_ref, new_sol_ref, new_res_ref, new_dir_ref):
    rhs = sol_ref.shape[0]
    even = lax.axis_index("side") == 0
    quarters = [jnp.where(even, mine_ref[n], other_ref[n]) for n in range(3)]
    quarters += [jnp.where(even, other_ref[n], mine_ref[n]) for n in range(3)]
    first, second = unpack_gram([jnp.concatenate(quarters[2 * n : 2 * n + 2], axis=0) for n in range(3)])
    for step in range(0, rhs, 4):
        first = eliminate(first, step)
        second = eliminate(second, step)
    alpha = first[:, 32:64]
    row = lax.broadcasted_iota(jnp.int32, (rhs, rhs), 0)
    col = lax.broadcasted_iota(jnp.int32, (rhs, rhs), 1)
    eye = (row == col).astype(F32)
    beta = eye - first[:, 64:96] + dot_f32(first[:, 96:128] - second[:, 32:64], alpha, ((1,), (0,)))
    direction = dir_ref[...]
    new_sol_ref[...] = sol_ref[...] + dot_f32(alpha, direction, ((0,), (0,)))
    new_res = res_ref[...] - dot_f32(alpha, image_ref[...], ((0,), (0,)))
    new_res_ref[...] = new_res
    new_dir_ref[...] = new_res + dot_f32(beta, direction, ((0,), (0,)))


def call(kernel, outs, ins, name, megabytes, scratch=(), space=pltpu.VMEM):
    return pl.pallas_call(
        kernel,
        out_shape=tuple(jax.ShapeDtypeStruct(*out) for out in outs),
        in_specs=[pl.BlockSpec(memory_space=space)] * len(ins),
        out_specs=(pl.BlockSpec(memory_space=pltpu.VMEM),) * len(outs),
        scratch_shapes=scratch,
        compiler_params=pltpu.CompilerParams(vmem_limit_bytes=megabytes << 20),
        name=name,
    )(*ins)


def per_device(chips, points, noise_var, district, solution, residual, direction):
    rhs, count = direction.shape
    whole_count = count * chips * 2
    group = ("row", "pair")
    swap = [(0, 1), (1, 0)]
    wide = ((rhs, count), F32)
    fetched = (points, district.reshape(1, count), noise_var.reshape(1, count), direction)
    fetched = tuple(pltpu.with_memory_space_constraint(arg, pltpu.HBM) for arg in fetched)
    block, own = call(
        pack_kernel,
        (((ROWS, LANES), BF16), ((8, count), F32)),
        fetched,
        "pack", 4,
        [pltpu.VMEM(arg.shape, arg.dtype) for arg in fetched] + [pltpu.SemaphoreType.DMA((len(fetched),))],
        pltpu.HBM,
    )
    near = lax.all_to_all(jnp.broadcast_to(block[None], (chips, ROWS, LANES)), group, 0, 0)
    far = lax.ppermute(near, "side", swap)
    product, sums, norm, side = call(
        first_kernel,
        (wide, ((rhs + 8, count), F32), ((rhs, LANES), F32), ((count, 40), BF16)),
        (own, direction, residual, near),
        "near_half", 24,
    )
    image, packed = call(
        functools.partial(second_kernel, whole_count),
        (wide, ((6, 4, LANES), F32)),
        (own, direction, residual, norm, product, sums, side, far),
        "far_half", 24,
    )
    copies = jnp.broadcast_to(packed.reshape(1, 2, 3, 4, LANES), (chips, 2, 3, 4, LANES)).reshape(-1, 3, 4, LANES)
    mine = jnp.sum(lax.all_to_all(copies, group + ("side",), 0, 0, tiled=True), axis=0)
    other = lax.ppermute(mine, "side", swap)
    return call(
        final_kernel,
        (wide,) * 3,
        (mine, other, solution, residual, direction, image),
        "final", 8,
    )


def solution(mesh):
    rows, cols = mesh.shape["row"], mesh.shape["col"]
    paired = Mesh(mesh.devices.reshape(rows, cols // 2, 2), ("row", "pair", "side"))
    samples = ("row", "pair", "side")
    wide, flat = P(None, samples), P(samples)
    return jax.shard_map(
        functools.partial(per_device, rows * cols // 2),
        mesh=paired,
        in_specs=(wide, flat, flat, wide, wide, wide),
        out_specs=(wide, wide, wide),
        check_vma=False,
    )
```

```python
import functools
import math

import jax
import jax.numpy as jnp
from jax import lax
from jax.experimental import pallas as pl
from jax.experimental.pallas import tpu as pltpu
from jax.sharding import Mesh, PartitionSpec as P

root_three = math.sqrt(3.0)
corr_range = 0.05
district_gain = 0.5
LANES = 128
ROWS = 72
F32, BF16 = jnp.float32, jnp.bfloat16


def dot_f32(left, right, dims):
    return lax.dot_general(
        left, right, (dims, ((), ())), precision=lax.Precision.HIGHEST, preferred_element_type=F32
    )


def dot_bf16(left, right, dims):
    return lax.dot_general(left, right, (dims, ((), ())), preferred_element_type=F32)


def three_pieces(vals):
    high = vals.astype(BF16)
    rest = vals - high.astype(F32)
    mid = rest.astype(BF16)
    low = (rest - mid.astype(F32)).astype(BF16)
    return high, mid, low


def stack_pieces(vals):
    rows, count = vals.shape
    ones = jnp.ones((LANES - 3 * rows, count), BF16)
    return jnp.concatenate([*three_pieces(vals), ones], axis=0)


def pack_kernel(
    points_hbm, dist_hbm, noise_hbm, dir_hbm, pack_ref, own_ref, points_ref, dist_ref, noise_ref, dir_ref, sems
):
    pairs = ((dir_hbm, dir_ref), (dist_hbm, dist_ref), (points_hbm, points_ref), (noise_hbm, noise_ref))
    copies = [pltpu.make_async_copy(src, dst, sems.at[n]) for n, (src, dst) in enumerate(pairs)]
    for copy in copies:
        copy.start()
    rhs, count = dir_ref.shape
    copies[1].wait()
    dist = dist_ref[...]
    first = dist[:, 0:1]
    last = dist[:, count - 1 : count]
    row = lax.broadcasted_iota(jnp.int32, (8, count), 0)
    picked = jnp.where(row == 0, first, last)
    wanted = (row == 0) | ((row == 1) & (first != last))
    mask = (wanted & (dist == picked)).astype(F32).astype(BF16)
    for copy in (copies[0], copies[2], copies[3]):
        copy.wait()
    pts = points_ref[...].astype(F32)
    own_ref[...] = jnp.concatenate(
        [pts, dist.astype(F32), noise_ref[...], jnp.zeros((4, count), F32)], axis=0
    )
    high, mid, low = three_pieces(dir_ref[...])
    ones = jnp.ones((LANES - 3 * rhs, count), BF16)
    edge = dot_bf16(mask, jnp.concatenate([high, high, high, ones], axis=0), ((1,), (1,)))
    edge = edge + dot_bf16(mask, jnp.concatenate([mid, mid, mid, 0 * ones], axis=0), ((1,), (1,)))
    edge = edge + dot_bf16(mask, jnp.concatenate([low, low, low, 0 * ones], axis=0), ((1,), (1,)))
    e_high, e_mid, e_low = (piece.astype(F32) for piece in three_pieces(edge))
    lane = lax.broadcasted_iota(jnp.int32, (8, LANES), 1)
    row8 = lax.broadcasted_iota(jnp.int32, (8, LANES), 0)
    label = jnp.where(row8 == 0, first, last).astype(F32)
    extras = jnp.where(lane < rhs, e_high, jnp.where(lane < 2 * rhs, e_mid, e_low))
    extras = jnp.where(lane == 3 * rhs, label, jnp.where(lane > 3 * rhs, edge, extras))
    tail = jnp.concatenate(
        [pts[:, 0:LANES], pts[:, LANES:], extras[0:2, :], jnp.zeros((2, LANES), F32)], axis=0
    )
    pack_ref[0:rhs, :] = high[:, 0:LANES]
    pack_ref[rhs : 2 * rhs, :] = high[:, LANES:]
    pack_ref[2 * rhs :, :] = tail.astype(BF16)


def own_side(own):
    scale = 3.0 / corr_range**2
    row = lax.broadcasted_iota(jnp.int32, own.shape, 0)
    cross = jnp.where(row < 2, own * (-2.0 * scale), 0.0)
    square = own * own
    norm = scale * (square[0:1] + square[1:2])
    cross_high, cross_low, _ = three_pieces(cross)
    high, mid, low = (piece.astype(F32) for piece in three_pieces(norm))
    ones = jnp.where(row < 2, scale, 0.0)
    norms = jnp.where(row == 0, high, jnp.where(row == 1, mid, jnp.where(row == 2, low, 0.0)))
    return jnp.concatenate([cross_high.astype(F32), cross_low.astype(F32), ones, ones, norms], axis=0)


def other_side(tail):
    left = tail.astype(F32)
    right = pltpu.roll(left, left.shape[0] - 2, 0)
    coords = jnp.concatenate([left, right], axis=1)
    square = coords * coords
    high = square.astype(BF16).astype(F32)
    return jnp.concatenate([coords, coords, high, square - high, jnp.ones_like(coords)], axis=0).astype(BF16)


def half_product(skip, own_ref, all_ref, side):
    blocks = all_ref.shape[0]
    count = own_ref.shape[1]
    rhs = 32
    to_two = -math.log2(math.e)

    def one_block(index, acc):
        block = all_ref[index]
        square = dot_bf16(side[...], other_side(block[2 * rhs :, :]), ((1,), (0,)))
        square = jnp.maximum(square, 1e-30)
        scaled = square * lax.rsqrt(square)
        tile = ((1.0 + scaled) * jnp.exp2(scaled * to_two)).astype(BF16)
        left = jnp.concatenate([block[0:rhs, :], block[rhs : 2 * rhs, :]], axis=1)
        return acc + dot_bf16(left, tile, ((1,), (1,)))

    def some_blocks(index, acc):
        for inner in range(batch):
            acc = one_block(index * batch + inner, acc)
        return acc

    batch = math.gcd(blocks, 16)
    product = jnp.zeros((rhs, count), F32)
    if blocks == batch:
        product = some_blocks(0, product)
    else:
        product = lax.fori_loop(0, blocks // batch, some_blocks, product)

    edges = all_ref[:, 2 * rhs :, :].astype(F32).reshape(blocks * 8, LANES)
    place = lax.broadcasted_iota(jnp.int32, (blocks * 8, count), 0)
    kind = place % 8
    good = ((kind == 4) | (kind == 5)) & (place // 8 != skip)
    match = good & (edges[:, 3 * rhs : 3 * rhs + 1] == own_ref[2:3, :])
    sums = dot_bf16(edges.astype(BF16), match.astype(F32).astype(BF16), ((0,), (0,)))
    extra = sums[0:rhs] + sums[rhs : 2 * rhs] + sums[2 * rhs : 3 * rhs]
    return product, extra, sums[3 * rhs + 1 : 3 * rhs + 2]


def first_kernel(own_ref, dir_ref, res_ref, all_ref, product_ref, sums_ref, norm_ref, side_ref):
    rhs, count = dir_ref.shape
    side_ref[...] = own_side(own_ref[...]).T.astype(BF16)
    product, extra, number = half_product(lax.axis_index(("row", "pair")), own_ref, all_ref, side_ref)
    product_ref[...] = product
    labels = lax.broadcasted_iota(jnp.int32, (64, count), 0).astype(F32)
    onehot = (labels == own_ref[2:3, :]).astype(F32).astype(BF16)
    same = dot_bf16(onehot, onehot, ((0,), (0,))).astype(BF16)
    sums = dot_bf16(stack_pieces(dir_ref[...]), same, ((1,), (0,)))
    sums_ref[0:rhs, :] = sums[0:rhs] + sums[rhs : 2 * rhs] + sums[2 * rhs : 3 * rhs] + extra
    sums_ref[rhs:, :] = sums[3 * rhs : 3 * rhs + 8] + number
    residual = res_ref[...]
    norm_ref[...] = jnp.zeros_like(norm_ref)
    norm_ref[:, 32:64] = dot_f32(residual, residual, ((1,), (1,)))


def second_kernel(
    whole_count, own_ref, dir_ref, res_ref, norm_ref, product_ref, sums_ref, side_ref, all_ref,
    image_ref, packed_ref,
):
    product, extra, number = half_product(-1, own_ref, all_ref, side_ref)
    product = product + product_ref[...]
    size = sums_ref[32:33, :] + number
    district_part = (sums_ref[0:32, :] + extra) / jnp.sqrt(size)
    direction = dir_ref[...]
    kernel_scale = 1.0 / (corr_range * math.sqrt(whole_count))
    image = own_ref[3:4, :] * direction + product * kernel_scale + district_gain * district_part
    image_ref[...] = image
    part = 0.5 * direction
    none = jnp.zeros_like(part)
    gram = dot_f32(image, jnp.concatenate([part, none, res_ref[...], image], axis=0), ((1,), (1,)))
    gram = gram + dot_f32(part, jnp.concatenate([image, none, none, none], axis=0), ((1,), (1,)))
    gram = gram + norm_ref[...]
    packed = pack_gram(gram)
    for n in range(6):
        packed_ref[n] = packed[n // 2][4 * (n % 2) : 4 * (n % 2) + 4, :]


def lane_groups(height):
    row = lax.broadcasted_iota(jnp.int32, (height, LANES), 0)
    lane = lax.broadcasted_iota(jnp.int32, (height, LANES), 1)
    return row, lane % 32, lane // 32


def pack_gram(gram):
    row, col, group = lane_groups(32)
    below = (col <= row) & (group <= 1)
    kept = jnp.where(below | (group == 2) | ((group == 3) & (col > row)), gram, 0.0)
    diag = jnp.sum(jnp.where((group == 3) & (col == row), gram, 0.0), axis=0, keepdims=True)
    diag = jnp.broadcast_to(diag, (8, LANES))
    row8, col8, group8 = lane_groups(8)
    packed = [jnp.zeros((8, LANES), F32)] * 3
    for n in range(4):
        rows = kept[8 * n : 8 * n + 8]
        for source, target in ((0, 1), (1, 2), (2, 0), (3, 1)):
            turn = (n - source) % 4 * 32
            moved = pltpu.roll(rows, turn, 1) if turn else rows
            packed[target] = packed[target] + jnp.where(group8 == n, moved, 0.0)
    packed[2] = packed[2] + jnp.where((group8 == 0) & (row8 == 0) & (col8 > 0), pltpu.roll(diag, 32, 1), 0.0)
    packed[2] = packed[2] + jnp.where((group8 == 0) & (row8 == 1) & (col8 == 2), pltpu.roll(diag, 34, 1), 0.0)
    return packed


def unpack_gram(packed):
    _, _, group8 = lane_groups(8)
    parts = []
    for n in range(4):
        rows = jnp.zeros((8, LANES), F32)
        for source, target in ((0, 1), (1, 2), (2, 0), (3, 1)):
            turn = (source - n) % 4 * 32
            moved = pltpu.roll(packed[target], turn, 1) if turn else packed[target]
            rows = jnp.where(group8 == source, moved, rows)
        parts.append(rows)
    flat = jnp.concatenate(parts, axis=0)
    row, col, group = lane_groups(32)
    spread = jnp.concatenate([jnp.where(group == n, flat, 0.0) for n in range(4)], axis=0).T
    turned = (spread[0:32] + spread[32:64]) + (spread[64:96] + spread[96:128])
    diag = jnp.where(col[0:1] == 0, pltpu.roll(flat[0:8], 62, 1)[1:2], pltpu.roll(flat[0:8], 64, 1)[0:1])
    direct = (group == 2) | ((group <= 1) & (col <= row)) | ((group == 3) & (col > row))
    first = jnp.where(direct, flat, jnp.where((group == 3) & (col == row), diag, turned))
    return first, jnp.where(group == 1, first, turned)


def solve_pair(a, b, c, d):
    inverse = 1.0 / a
    lower = c * inverse
    inverse_rest = 1.0 / (d - lower * b)

    def solve(top, bottom):
        second = (bottom - lower * top) * inverse_rest
        return (top - b * second) * inverse, second

    return solve


def eliminate(work, step, at):
    rows = lax.broadcasted_iota(jnp.int32, work.shape, 0)
    cols = [jnp.broadcast_to(work[:, at + step + n : at + step + n + 1], work.shape) for n in range(4)]
    line = [work[step + n : step + n + 1, :] for n in range(4)]
    piv = [[cols[m][step + n : step + n + 1, :] for m in range(4)] for n in range(4)]
    first_block = solve_pair(piv[0][0], piv[0][1], piv[1][0], piv[1][1])
    new0, new1 = first_block(line[0], line[1])
    cross = [first_block(piv[0][m], piv[1][m]) for m in (2, 3)]
    rest = [[piv[n][m + 2] - piv[n][0] * cross[m][0] - piv[n][1] * cross[m][1] for m in range(2)] for n in (2, 3)]
    left2 = line[2] - piv[2][0] * new0 - piv[2][1] * new1
    left3 = line[3] - piv[3][0] * new0 - piv[3][1] * new1
    new2, new3 = solve_pair(rest[0][0], rest[0][1], rest[1][0], rest[1][1])(left2, left3)
    new0 = new0 - cross[0][0] * new2 - cross[1][0] * new3
    new1 = new1 - cross[0][1] * new2 - cross[1][1] * new3
    work = work - (cols[0] * new0 + cols[1] * new1) - (cols[2] * new2 + cols[3] * new3)
    for n, new in enumerate((new0, new1, new2, new3)):
        work = jnp.where(rows == step + n, new, work)
    return work


def final_kernel(mine_ref, other_ref, sol_ref, res_ref, dir_ref, image_ref, new_sol_ref, new_res_ref, new_dir_ref):
    rhs = sol_ref.shape[0]
    even = lax.axis_index("side") == 0
    quarters = [jnp.where(even, mine_ref[n], other_ref[n]) for n in range(3)]
    quarters += [jnp.where(even, other_ref[n], mine_ref[n]) for n in range(3)]
    first, second = unpack_gram([jnp.concatenate(quarters[2 * n : 2 * n + 2], axis=0) for n in range(3)])
    for step in range(0, rhs, 4):
        first = eliminate(first, step, 0)
        second = eliminate(second, step, rhs)
    alpha = first[:, 32:64]
    row = lax.broadcasted_iota(jnp.int32, (rhs, rhs), 0)
    col = lax.broadcasted_iota(jnp.int32, (rhs, rhs), 1)
    eye = (row == col).astype(F32)
    beta = eye - first[:, 64:96] + dot_f32(first[:, 96:128] - second[:, 64:96], alpha, ((1,), (0,)))
    direction = dir_ref[...]
    new_sol_ref[...] = sol_ref[...] + dot_f32(alpha, direction, ((0,), (0,)))
    new_res = res_ref[...] - dot_f32(alpha, image_ref[...], ((0,), (0,)))
    new_res_ref[...] = new_res
    new_dir_ref[...] = new_res + dot_f32(beta, direction, ((0,), (0,)))


def call(kernel, outs, ins, name, megabytes, scratch=(), space=pltpu.VMEM):
    return pl.pallas_call(
        kernel,
        out_shape=tuple(jax.ShapeDtypeStruct(*out) for out in outs),
        in_specs=[pl.BlockSpec(memory_space=space)] * len(ins),
        out_specs=(pl.BlockSpec(memory_space=pltpu.VMEM),) * len(outs),
        scratch_shapes=scratch,
        compiler_params=pltpu.CompilerParams(vmem_limit_bytes=megabytes << 20),
        name=name,
    )(*ins)


def per_device(chips, points, noise_var, district, solution, residual, direction):
    rhs, count = direction.shape
    whole_count = count * chips * 2
    group = ("row", "pair")
    swap = [(0, 1), (1, 0)]
    wide = ((rhs, count), F32)
    fetched = (points, district.reshape(1, count), noise_var.reshape(1, count), direction)
    fetched = tuple(pltpu.with_memory_space_constraint(arg, pltpu.HBM) for arg in fetched)
    block, own = call(
        pack_kernel,
        (((ROWS, LANES), BF16), ((8, count), F32)),
        fetched,
        "pack", 4,
        [pltpu.VMEM(arg.shape, arg.dtype) for arg in fetched] + [pltpu.SemaphoreType.DMA((len(fetched),))],
        pltpu.HBM,
    )
    near = lax.all_to_all(jnp.broadcast_to(block[None], (chips, ROWS, LANES)), group, 0, 0)
    far = lax.ppermute(near, "side", swap)
    product, sums, norm, side = call(
        first_kernel,
        (wide, ((rhs + 8, count), F32), ((rhs, LANES), F32), ((count, 40), BF16)),
        (own, direction, residual, near),
        "near_half", 24,
    )
    image, packed = call(
        functools.partial(second_kernel, whole_count),
        (wide, ((6, 4, LANES), F32)),
        (own, direction, residual, norm, product, sums, side, far),
        "far_half", 24,
    )
    copies = jnp.broadcast_to(packed.reshape(1, 2, 3, 4, LANES), (chips, 2, 3, 4, LANES)).reshape(-1, 3, 4, LANES)
    mine = jnp.sum(lax.all_to_all(copies, group + ("side",), 0, 0, tiled=True), axis=0)
    other = lax.ppermute(mine, "side", swap)
    return call(
        final_kernel,
        (wide,) * 3,
        (mine, other, solution, residual, direction, image),
        "final", 8,
    )


def solution(mesh):
    rows, cols = mesh.shape["row"], mesh.shape["col"]
    paired = Mesh(mesh.devices.reshape(rows, cols // 2, 2), ("row", "pair", "side"))
    samples = ("row", "pair", "side")
    wide, flat = P(None, samples), P(samples)
    return jax.shard_map(
        functools.partial(per_device, rows * cols // 2),
        mesh=paired,
        in_specs=(wide, flat, flat, wide, wide, wide),
        out_specs=(wide, wide, wide),
        check_vma=False,
    )
```

```python
import functools
import math

import jax
import jax.numpy as jnp
from jax import lax
from jax.experimental import pallas as pl
from jax.experimental.pallas import tpu as pltpu
from jax.sharding import Mesh, PartitionSpec as P

root_three = math.sqrt(3.0)
corr_range = 0.05
district_gain = 0.5
LANES = 128
ROWS = 72
F32, BF16 = jnp.float32, jnp.bfloat16


def dot_f32(left, right, dims):
    return lax.dot_general(
        left, right, (dims, ((), ())), precision=lax.Precision.HIGHEST, preferred_element_type=F32
    )


def dot_bf16(left, right, dims):
    return lax.dot_general(left, right, (dims, ((), ())), preferred_element_type=F32)


def three_pieces(vals):
    high = vals.astype(BF16)
    rest = vals - high.astype(F32)
    mid = rest.astype(BF16)
    low = (rest - mid.astype(F32)).astype(BF16)
    return high, mid, low


def stack_pieces(vals):
    rows, count = vals.shape
    ones = jnp.ones((LANES - 3 * rows, count), BF16)
    return jnp.concatenate([*three_pieces(vals), ones], axis=0)


def pack_kernel(
    points_hbm, dist_hbm, noise_hbm, dir_hbm, pack_ref, own_ref, points_ref, dist_ref, noise_ref, dir_ref, sems
):
    pairs = ((dir_hbm, dir_ref), (dist_hbm, dist_ref), (points_hbm, points_ref), (noise_hbm, noise_ref))
    copies = [pltpu.make_async_copy(src, dst, sems.at[n]) for n, (src, dst) in enumerate(pairs)]
    for copy in copies:
        copy.start()
    rhs, count = dir_ref.shape
    copies[1].wait()
    dist = dist_ref[...]
    first = dist[:, 0:1]
    last = dist[:, count - 1 : count]
    row = lax.broadcasted_iota(jnp.int32, (8, count), 0)
    picked = jnp.where(row == 0, first, last)
    wanted = (row == 0) | ((row == 1) & (first != last))
    mask = (wanted & (dist == picked)).astype(F32).astype(BF16)
    for copy in (copies[0], copies[2], copies[3]):
        copy.wait()
    pts = points_ref[...].astype(F32)
    own_ref[...] = jnp.concatenate(
        [pts, dist.astype(F32), noise_ref[...], jnp.zeros((4, count), F32)], axis=0
    )
    high, mid, low = three_pieces(dir_ref[...])
    ones = jnp.ones((LANES - 3 * rhs, count), BF16)
    edge = dot_bf16(mask, jnp.concatenate([high, high, high, ones], axis=0), ((1,), (1,)))
    edge = edge + dot_bf16(mask, jnp.concatenate([mid, mid, mid, 0 * ones], axis=0), ((1,), (1,)))
    edge = edge + dot_bf16(mask, jnp.concatenate([low, low, low, 0 * ones], axis=0), ((1,), (1,)))
    e_high, e_mid, e_low = (piece.astype(F32) for piece in three_pieces(edge))
    lane = lax.broadcasted_iota(jnp.int32, (8, LANES), 1)
    row8 = lax.broadcasted_iota(jnp.int32, (8, LANES), 0)
    label = jnp.where(row8 == 0, first, last).astype(F32)
    extras = jnp.where(lane < rhs, e_high, jnp.where(lane < 2 * rhs, e_mid, e_low))
    extras = jnp.where(lane == 3 * rhs, label, jnp.where(lane > 3 * rhs, edge, extras))
    tail = jnp.concatenate(
        [pts[:, 0:LANES], pts[:, LANES:], extras[0:2, :], jnp.zeros((2, LANES), F32)], axis=0
    )
    pack_ref[0:rhs, :] = high[:, 0:LANES]
    pack_ref[rhs : 2 * rhs, :] = high[:, LANES:]
    pack_ref[2 * rhs :, :] = tail.astype(BF16)


def own_side(own):
    scale = 3.0 / corr_range**2
    row = lax.broadcasted_iota(jnp.int32, own.shape, 0)
    cross = jnp.where(row < 2, own * (-2.0 * scale), 0.0)
    square = own * own
    norm = scale * (square[0:1] + square[1:2])
    cross_high, cross_low, _ = three_pieces(cross)
    high, mid, low = (piece.astype(F32) for piece in three_pieces(norm))
    ones = jnp.where(row < 2, scale, 0.0)
    norms = jnp.where(row == 0, high, jnp.where(row == 1, mid, jnp.where(row == 2, low, 0.0)))
    return jnp.concatenate([cross_high.astype(F32), cross_low.astype(F32), ones, ones, norms], axis=0)


def other_side(tail):
    left = tail.astype(F32)
    right = pltpu.roll(left, left.shape[0] - 2, 0)
    coords = jnp.concatenate([left, right], axis=1)
    square = coords * coords
    high = square.astype(BF16).astype(F32)
    return jnp.concatenate([coords, coords, high, square - high, jnp.ones_like(coords)], axis=0).astype(BF16)


def half_product(skip, own_ref, all_ref, side):
    blocks = all_ref.shape[0]
    count = own_ref.shape[1]
    rhs = 32
    to_two = -math.log2(math.e)

    def one_block(index, acc):
        block = all_ref[index]
        square = dot_bf16(side[...], other_side(block[2 * rhs :, :]), ((1,), (0,)))
        square = jnp.maximum(square, 1e-30)
        scaled = square * lax.rsqrt(square)
        tile = ((1.0 + scaled) * jnp.exp2(scaled * to_two)).astype(BF16)
        left = jnp.concatenate([block[0:rhs, :], block[rhs : 2 * rhs, :]], axis=1)
        return acc + dot_bf16(left, tile, ((1,), (1,)))

    def some_blocks(index, acc):
        for inner in range(batch):
            acc = one_block(index * batch + inner, acc)
        return acc

    batch = math.gcd(blocks, 16)
    product = jnp.zeros((rhs, count), F32)
    if blocks == batch:
        product = some_blocks(0, product)
    else:
        product = lax.fori_loop(0, blocks // batch, some_blocks, product)

    edges = all_ref[:, 2 * rhs :, :].astype(F32).reshape(blocks * 8, LANES)
    place = lax.broadcasted_iota(jnp.int32, (blocks * 8, count), 0)
    kind = place % 8
    good = ((kind == 4) | (kind == 5)) & (place // 8 != skip)
    match = good & (edges[:, 3 * rhs : 3 * rhs + 1] == own_ref[2:3, :])
    sums = dot_bf16(edges.astype(BF16), match.astype(F32).astype(BF16), ((0,), (0,)))
    extra = sums[0:rhs] + sums[rhs : 2 * rhs] + sums[2 * rhs : 3 * rhs]
    return product, extra, sums[3 * rhs + 1 : 3 * rhs + 2]


def first_kernel(own_ref, dir_ref, res_ref, all_ref, product_ref, sums_ref, norm_ref, side_ref):
    rhs, count = dir_ref.shape
    side_ref[...] = own_side(own_ref[...]).T.astype(BF16)
    product, extra, number = half_product(lax.axis_index(("row", "pair")), own_ref, all_ref, side_ref)
    product_ref[...] = product
    labels = lax.broadcasted_iota(jnp.int32, (64, count), 0).astype(F32)
    onehot = (labels == own_ref[2:3, :]).astype(F32).astype(BF16)
    same = dot_bf16(onehot, onehot, ((0,), (0,))).astype(BF16)
    sums = dot_bf16(stack_pieces(dir_ref[...]), same, ((1,), (0,)))
    sums_ref[0:rhs, :] = sums[0:rhs] + sums[rhs : 2 * rhs] + sums[2 * rhs : 3 * rhs] + extra
    sums_ref[rhs:, :] = sums[3 * rhs : 3 * rhs + 8] + number
    residual = res_ref[...]
    norm_ref[...] = jnp.zeros_like(norm_ref)
    norm_ref[:, 32:64] = dot_f32(residual, residual, ((1,), (1,)))


def second_kernel(
    whole_count, own_ref, dir_ref, res_ref, norm_ref, product_ref, sums_ref, side_ref, all_ref,
    image_ref, packed_ref,
):
    product, extra, number = half_product(-1, own_ref, all_ref, side_ref)
    product = product + product_ref[...]
    size = sums_ref[32:33, :] + number
    district_part = (sums_ref[0:32, :] + extra) / jnp.sqrt(size)
    direction = dir_ref[...]
    kernel_scale = 1.0 / (corr_range * math.sqrt(whole_count))
    image = own_ref[3:4, :] * direction + product * kernel_scale + district_gain * district_part
    image_ref[...] = image
    part = 0.5 * direction
    none = jnp.zeros_like(part)
    gram = dot_f32(image, jnp.concatenate([part, none, res_ref[...], image], axis=0), ((1,), (1,)))
    gram = gram + dot_f32(part, jnp.concatenate([image, none, none, none], axis=0), ((1,), (1,)))
    gram = gram + norm_ref[...]
    packed = pack_gram(gram)
    for n in range(6):
        packed_ref[n] = packed[n // 2][4 * (n % 2) : 4 * (n % 2) + 4, :]


def lane_groups(height):
    row = lax.broadcasted_iota(jnp.int32, (height, LANES), 0)
    lane = lax.broadcasted_iota(jnp.int32, (height, LANES), 1)
    return row, lane % 32, lane // 32


def pack_gram(gram):
    row, col, group = lane_groups(32)
    below = (col <= row) & (group <= 1)
    kept = jnp.where(below | (group == 2) | ((group == 3) & (col > row)), gram, 0.0)
    diag = jnp.sum(jnp.where((group == 3) & (col == row), gram, 0.0), axis=0, keepdims=True)
    diag = jnp.broadcast_to(diag, (8, LANES))
    row8, col8, group8 = lane_groups(8)
    packed = [jnp.zeros((8, LANES), F32)] * 3
    for n in range(4):
        rows = kept[8 * n : 8 * n + 8]
        for source, target in ((0, 1), (1, 2), (2, 0), (3, 1)):
            turn = (n - source) % 4 * 32
            moved = pltpu.roll(rows, turn, 1) if turn else rows
            packed[target] = packed[target] + jnp.where(group8 == n, moved, 0.0)
    packed[2] = packed[2] + jnp.where((group8 == 0) & (row8 == 0) & (col8 > 0), pltpu.roll(diag, 32, 1), 0.0)
    packed[2] = packed[2] + jnp.where((group8 == 0) & (row8 == 1) & (col8 == 2), pltpu.roll(diag, 34, 1), 0.0)
    return packed


def unpack_gram(packed):
    _, _, group8 = lane_groups(8)
    parts = []
    for n in range(4):
        rows = jnp.zeros((8, LANES), F32)
        for source, target in ((0, 1), (1, 2), (2, 0), (3, 1)):
            turn = (source - n) % 4 * 32
            moved = pltpu.roll(packed[target], turn, 1) if turn else packed[target]
            rows = jnp.where(group8 == source, moved, rows)
        parts.append(rows)
    flat = jnp.concatenate(parts, axis=0)
    row, col, group = lane_groups(32)
    spread = jnp.concatenate([jnp.where(group == n, flat, 0.0) for n in range(4)], axis=0).T
    turned = (spread[0:32] + spread[32:64]) + (spread[64:96] + spread[96:128])
    diag = jnp.where(col[0:1] == 0, pltpu.roll(flat[0:8], 62, 1)[1:2], pltpu.roll(flat[0:8], 64, 1)[0:1])
    direct = (group == 2) | ((group <= 1) & (col <= row)) | ((group == 3) & (col > row))
    first = jnp.where(direct, flat, jnp.where((group == 3) & (col == row), diag, turned))
    return first, jnp.where(group == 1, first, turned)


def solve_pair(a, b, c, d):
    inverse = 1.0 / a
    lower = c * inverse
    inverse_rest = 1.0 / (d - lower * b)

    def solve(top, bottom):
        second = (bottom - lower * top) * inverse_rest
        return (top - b * second) * inverse, second

    return solve


def eliminate(work, step, at):
    rows = lax.broadcasted_iota(jnp.int32, work.shape, 0)
    cols = [jnp.broadcast_to(work[:, at + step + n : at + step + n + 1], work.shape) for n in range(4)]
    line = [work[step + n : step + n + 1, :] for n in range(4)]
    piv = [[cols[m][step + n : step + n + 1, :] for m in range(4)] for n in range(4)]
    first_block = solve_pair(piv[0][0], piv[0][1], piv[1][0], piv[1][1])
    new0, new1 = first_block(line[0], line[1])
    cross = [first_block(piv[0][m], piv[1][m]) for m in (2, 3)]
    rest = [[piv[n][m + 2] - piv[n][0] * cross[m][0] - piv[n][1] * cross[m][1] for m in range(2)] for n in (2, 3)]
    left2 = line[2] - piv[2][0] * new0 - piv[2][1] * new1
    left3 = line[3] - piv[3][0] * new0 - piv[3][1] * new1
    new2, new3 = solve_pair(rest[0][0], rest[0][1], rest[1][0], rest[1][1])(left2, left3)
    new0 = new0 - cross[0][0] * new2 - cross[1][0] * new3
    new1 = new1 - cross[0][1] * new2 - cross[1][1] * new3
    work = work - (cols[0] * new0 + cols[1] * new1) - (cols[2] * new2 + cols[3] * new3)
    for n, new in enumerate((new0, new1, new2, new3)):
        work = jnp.where(rows == step + n, new, work)
    return work


def spread_left(vals):
    high, mid, low = (piece.astype(F32) for piece in three_pieces(vals))
    return jnp.concatenate([high, high, mid, high, mid, low], axis=0).astype(BF16)


def spread_right(vals):
    high, mid, low = three_pieces(vals)
    return jnp.concatenate([high, mid, high, low, mid, high], axis=0)


def final_kernel(mine_ref, other_ref, sol_ref, res_ref, dir_ref, image_ref, new_sol_ref, new_res_ref, new_dir_ref):
    rhs = sol_ref.shape[0]
    even = lax.axis_index("side") == 0
    quarters = [jnp.where(even, mine_ref[n], other_ref[n]) for n in range(3)]
    quarters += [jnp.where(even, other_ref[n], mine_ref[n]) for n in range(3)]
    first, second = unpack_gram([jnp.concatenate(quarters[2 * n : 2 * n + 2], axis=0) for n in range(3)])
    for step in range(0, rhs, 4):
        first = eliminate(first, step, 0)
        second = eliminate(second, step, rhs)
    alpha = first[:, 32:64]
    row = lax.broadcasted_iota(jnp.int32, (rhs, rhs), 0)
    col = lax.broadcasted_iota(jnp.int32, (rhs, rhs), 1)
    eye = (row == col).astype(F32)
    beta = eye - first[:, 64:96] + dot_f32(first[:, 96:128] - second[:, 64:96], alpha, ((1,), (0,)))
    direction, image = spread_right(dir_ref[...]), spread_right(image_ref[...])
    spread_alpha = spread_left(alpha)
    new_sol_ref[...] = sol_ref[...] + dot_bf16(spread_alpha, direction, ((0,), (0,)))
    new_res = res_ref[...] - dot_bf16(spread_alpha, image, ((0,), (0,)))
    new_res_ref[...] = new_res
    new_dir_ref[...] = new_res + dot_bf16(spread_left(beta), direction, ((0,), (0,)))


def call(kernel, outs, ins, name, megabytes, scratch=(), space=pltpu.VMEM):
    return pl.pallas_call(
        kernel,
        out_shape=tuple(jax.ShapeDtypeStruct(*out) for out in outs),
        in_specs=[pl.BlockSpec(memory_space=space)] * len(ins),
        out_specs=(pl.BlockSpec(memory_space=pltpu.VMEM),) * len(outs),
        scratch_shapes=scratch,
        compiler_params=pltpu.CompilerParams(vmem_limit_bytes=megabytes << 20),
        name=name,
    )(*ins)


def per_device(chips, points, noise_var, district, solution, residual, direction):
    rhs, count = direction.shape
    whole_count = count * chips * 2
    group = ("row", "pair")
    swap = [(0, 1), (1, 0)]
    wide = ((rhs, count), F32)
    fetched = (points, district.reshape(1, count), noise_var.reshape(1, count), direction)
    fetched = tuple(pltpu.with_memory_space_constraint(arg, pltpu.HBM) for arg in fetched)
    block, own = call(
        pack_kernel,
        (((ROWS, LANES), BF16), ((8, count), F32)),
        fetched,
        "pack", 4,
        [pltpu.VMEM(arg.shape, arg.dtype) for arg in fetched] + [pltpu.SemaphoreType.DMA((len(fetched),))],
        pltpu.HBM,
    )
    near = lax.all_to_all(jnp.broadcast_to(block[None], (chips, ROWS, LANES)), group, 0, 0)
    far = lax.ppermute(near, "side", swap)
    product, sums, norm, side = call(
        first_kernel,
        (wide, ((rhs + 8, count), F32), ((rhs, LANES), F32), ((count, 40), BF16)),
        (own, direction, residual, near),
        "near_half", 24,
    )
    image, packed = call(
        functools.partial(second_kernel, whole_count),
        (wide, ((6, 4, LANES), F32)),
        (own, direction, residual, norm, product, sums, side, far),
        "far_half", 24,
    )
    copies = jnp.broadcast_to(packed.reshape(1, 2, 3, 4, LANES), (chips, 2, 3, 4, LANES)).reshape(-1, 3, 4, LANES)
    mine = jnp.sum(lax.all_to_all(copies, group + ("side",), 0, 0, tiled=True), axis=0)
    other = lax.ppermute(mine, "side", swap)
    return call(
        final_kernel,
        (wide,) * 3,
        (mine, other, solution, residual, direction, image),
        "final", 8,
    )


def solution(mesh):
    rows, cols = mesh.shape["row"], mesh.shape["col"]
    paired = Mesh(mesh.devices.reshape(rows, cols // 2, 2), ("row", "pair", "side"))
    samples = ("row", "pair", "side")
    wide, flat = P(None, samples), P(samples)
    return jax.shard_map(
        functools.partial(per_device, rows * cols // 2),
        mesh=paired,
        in_specs=(wide, flat, flat, wide, wide, wide),
        out_specs=(wide, wide, wide),
        check_vma=False,
    )
```

```python
import functools
import math

import jax
import jax.numpy as jnp
from jax import lax
from jax.experimental import pallas as pl
from jax.experimental.pallas import tpu as pltpu
from jax.sharding import Mesh, PartitionSpec as P

root_three = math.sqrt(3.0)
corr_range = 0.05
district_gain = 0.5
LANES = 128
ROWS = 72
F32, BF16 = jnp.float32, jnp.bfloat16


def dot_f32(left, right, dims):
    return lax.dot_general(
        left, right, (dims, ((), ())), precision=lax.Precision.HIGHEST, preferred_element_type=F32
    )


def dot_bf16(left, right, dims):
    return lax.dot_general(left, right, (dims, ((), ())), preferred_element_type=F32)


def three_pieces(vals):
    high = vals.astype(BF16)
    rest = vals - high.astype(F32)
    mid = rest.astype(BF16)
    low = (rest - mid.astype(F32)).astype(BF16)
    return high, mid, low


def stack_pieces(vals):
    rows, count = vals.shape
    ones = jnp.ones((LANES - 3 * rows, count), BF16)
    return jnp.concatenate([*three_pieces(vals), ones], axis=0)


def pack_kernel(
    points_hbm, dist_hbm, noise_hbm, dir_hbm, pack_ref, own_ref, points_ref, dist_ref, noise_ref, dir_ref, sems
):
    pairs = ((dir_hbm, dir_ref), (dist_hbm, dist_ref), (points_hbm, points_ref), (noise_hbm, noise_ref))
    copies = [pltpu.make_async_copy(src, dst, sems.at[n]) for n, (src, dst) in enumerate(pairs)]
    for copy in copies:
        copy.start()
    rhs, count = dir_ref.shape
    copies[1].wait()
    dist = dist_ref[...]
    first = dist[:, 0:1]
    last = dist[:, count - 1 : count]
    row = lax.broadcasted_iota(jnp.int32, (8, count), 0)
    picked = jnp.where(row == 0, first, last)
    wanted = (row == 0) | ((row == 1) & (first != last))
    mask = (wanted & (dist == picked)).astype(F32).astype(BF16)
    for copy in (copies[0], copies[2], copies[3]):
        copy.wait()
    pts = points_ref[...].astype(F32)
    own_ref[...] = jnp.concatenate(
        [pts, dist.astype(F32), noise_ref[...], jnp.zeros((4, count), F32)], axis=0
    )
    high, mid, low = three_pieces(dir_ref[...])
    ones = jnp.ones((LANES - 3 * rhs, count), BF16)
    edge = dot_bf16(mask, jnp.concatenate([high, high, high, ones], axis=0), ((1,), (1,)))
    edge = edge + dot_bf16(mask, jnp.concatenate([mid, mid, mid, 0 * ones], axis=0), ((1,), (1,)))
    edge = edge + dot_bf16(mask, jnp.concatenate([low, low, low, 0 * ones], axis=0), ((1,), (1,)))
    e_high, e_mid, e_low = (piece.astype(F32) for piece in three_pieces(edge))
    lane = lax.broadcasted_iota(jnp.int32, (8, LANES), 1)
    row8 = lax.broadcasted_iota(jnp.int32, (8, LANES), 0)
    label = jnp.where(row8 == 0, first, last).astype(F32)
    extras = jnp.where(lane < rhs, e_high, jnp.where(lane < 2 * rhs, e_mid, e_low))
    extras = jnp.where(lane == 3 * rhs, label, jnp.where(lane > 3 * rhs, edge, extras))
    tail = jnp.concatenate(
        [pts[:, 0:LANES], pts[:, LANES:], extras[0:2, :], jnp.zeros((2, LANES), F32)], axis=0
    )
    pack_ref[0:rhs, :] = high[:, 0:LANES]
    pack_ref[rhs : 2 * rhs, :] = high[:, LANES:]
    pack_ref[2 * rhs :, :] = tail.astype(BF16)


def own_side(own):
    scale = 3.0 / corr_range**2
    row = lax.broadcasted_iota(jnp.int32, own.shape, 0)
    cross = jnp.where(row < 2, own * (-2.0 * scale), 0.0)
    square = own * own
    norm = scale * (square[0:1] + square[1:2])
    cross_high, cross_low, _ = three_pieces(cross)
    high, mid, low = (piece.astype(F32) for piece in three_pieces(norm))
    ones = jnp.where(row < 2, scale, 0.0)
    norms = jnp.where(row == 0, high, jnp.where(row == 1, mid, jnp.where(row == 2, low, 0.0)))
    return jnp.concatenate([cross_high.astype(F32), cross_low.astype(F32), ones, ones, norms], axis=0)


def other_side(tail):
    left = tail.astype(F32)
    right = pltpu.roll(left, left.shape[0] - 2, 0)
    coords = jnp.concatenate([left, right], axis=1)
    square = coords * coords
    high = square.astype(BF16).astype(F32)
    return jnp.concatenate([coords, coords, high, square - high, jnp.ones_like(coords)], axis=0).astype(BF16)


def half_product(skip, own_ref, all_ref, side):
    blocks = all_ref.shape[0]
    count = own_ref.shape[1]
    rhs = 32
    to_two = -math.log2(math.e)

    def one_block(index, acc):
        block = all_ref[index]
        square = dot_bf16(side[...], other_side(block[2 * rhs :, :]), ((1,), (0,)))
        square = jnp.maximum(square, 1e-30)
        scaled = square * lax.rsqrt(square)
        tile = ((1.0 + scaled) * jnp.exp2(scaled * to_two)).astype(BF16)
        left = jnp.concatenate([block[0:rhs, :], block[rhs : 2 * rhs, :]], axis=1)
        return acc + dot_bf16(left, tile, ((1,), (1,)))

    def some_blocks(index, acc):
        for inner in range(batch):
            acc = one_block(index * batch + inner, acc)
        return acc

    batch = math.gcd(blocks, 16)
    product = jnp.zeros((rhs, count), F32)
    if blocks == batch:
        product = some_blocks(0, product)
    else:
        product = lax.fori_loop(0, blocks // batch, some_blocks, product)

    edges = all_ref[:, 2 * rhs :, :].astype(F32).reshape(blocks * 8, LANES)
    place = lax.broadcasted_iota(jnp.int32, (blocks * 8, count), 0)
    kind = place % 8
    good = ((kind == 4) | (kind == 5)) & (place // 8 != skip)
    match = good & (edges[:, 3 * rhs : 3 * rhs + 1] == own_ref[2:3, :])
    sums = dot_bf16(edges.astype(BF16), match.astype(F32).astype(BF16), ((0,), (0,)))
    extra = sums[0:rhs] + sums[rhs : 2 * rhs] + sums[2 * rhs : 3 * rhs]
    return product, extra, sums[3 * rhs + 1 : 3 * rhs + 2]


def place_in_group(chips):
    place = lax.axis_index(("row", "pair"))
    return jnp.where(lax.axis_index("side") == 0, place, (place + chips // 2) % chips)


def first_kernel(own_ref, dir_ref, res_ref, all_ref, product_ref, sums_ref, norm_ref, side_ref):
    rhs, count = dir_ref.shape
    side_ref[...] = own_side(own_ref[...]).T.astype(BF16)
    product, extra, number = half_product(place_in_group(all_ref.shape[0]), own_ref, all_ref, side_ref)
    product_ref[...] = product
    labels = lax.broadcasted_iota(jnp.int32, (64, count), 0).astype(F32)
    onehot = (labels == own_ref[2:3, :]).astype(F32).astype(BF16)
    same = dot_bf16(onehot, onehot, ((0,), (0,))).astype(BF16)
    sums = dot_bf16(stack_pieces(dir_ref[...]), same, ((1,), (0,)))
    sums_ref[0:rhs, :] = sums[0:rhs] + sums[rhs : 2 * rhs] + sums[2 * rhs : 3 * rhs] + extra
    sums_ref[rhs:, :] = sums[3 * rhs : 3 * rhs + 8] + number
    residual = res_ref[...]
    norm_ref[...] = jnp.zeros_like(norm_ref)
    norm_ref[:, 32:64] = dot_f32(residual, residual, ((1,), (1,)))


def second_kernel(
    whole_count, own_ref, dir_ref, res_ref, norm_ref, product_ref, sums_ref, side_ref, all_ref,
    image_ref, packed_ref,
):
    product, extra, number = half_product(-1, own_ref, all_ref, side_ref)
    product = product + product_ref[...]
    size = sums_ref[32:33, :] + number
    district_part = (sums_ref[0:32, :] + extra) / jnp.sqrt(size)
    direction = dir_ref[...]
    kernel_scale = 1.0 / (corr_range * math.sqrt(whole_count))
    image = own_ref[3:4, :] * direction + product * kernel_scale + district_gain * district_part
    image_ref[...] = image
    part = 0.5 * direction
    none = jnp.zeros_like(part)
    gram = dot_f32(image, jnp.concatenate([part, none, res_ref[...], image], axis=0), ((1,), (1,)))
    gram = gram + dot_f32(part, jnp.concatenate([image, none, none, none], axis=0), ((1,), (1,)))
    gram = gram + norm_ref[...]
    packed = pack_gram(gram)
    for n in range(6):
        packed_ref[n] = packed[n // 2][4 * (n % 2) : 4 * (n % 2) + 4, :]


def lane_groups(height):
    row = lax.broadcasted_iota(jnp.int32, (height, LANES), 0)
    lane = lax.broadcasted_iota(jnp.int32, (height, LANES), 1)
    return row, lane % 32, lane // 32


def pack_gram(gram):
    row, col, group = lane_groups(32)
    below = (col <= row) & (group <= 1)
    kept = jnp.where(below | (group == 2) | ((group == 3) & (col > row)), gram, 0.0)
    diag = jnp.sum(jnp.where((group == 3) & (col == row), gram, 0.0), axis=0, keepdims=True)
    diag = jnp.broadcast_to(diag, (8, LANES))
    row8, col8, group8 = lane_groups(8)
    packed = [jnp.zeros((8, LANES), F32)] * 3
    for n in range(4):
        rows = kept[8 * n : 8 * n + 8]
        for source, target in ((0, 1), (1, 2), (2, 0), (3, 1)):
            turn = (n - source) % 4 * 32
            moved = pltpu.roll(rows, turn, 1) if turn else rows
            packed[target] = packed[target] + jnp.where(group8 == n, moved, 0.0)
    packed[2] = packed[2] + jnp.where((group8 == 0) & (row8 == 0) & (col8 > 0), pltpu.roll(diag, 32, 1), 0.0)
    packed[2] = packed[2] + jnp.where((group8 == 0) & (row8 == 1) & (col8 == 2), pltpu.roll(diag, 34, 1), 0.0)
    return packed


def unpack_gram(packed):
    _, _, group8 = lane_groups(8)
    parts = []
    for n in range(4):
        rows = jnp.zeros((8, LANES), F32)
        for source, target in ((0, 1), (1, 2), (2, 0), (3, 1)):
            turn = (source - n) % 4 * 32
            moved = pltpu.roll(packed[target], turn, 1) if turn else packed[target]
            rows = jnp.where(group8 == source, moved, rows)
        parts.append(rows)
    flat = jnp.concatenate(parts, axis=0)
    row, col, group = lane_groups(32)
    spread = jnp.concatenate([jnp.where(group == n, flat, 0.0) for n in range(4)], axis=0).T
    turned = (spread[0:32] + spread[32:64]) + (spread[64:96] + spread[96:128])
    diag = jnp.where(col[0:1] == 0, pltpu.roll(flat[0:8], 62, 1)[1:2], pltpu.roll(flat[0:8], 64, 1)[0:1])
    direct = (group == 2) | ((group <= 1) & (col <= row)) | ((group == 3) & (col > row))
    first = jnp.where(direct, flat, jnp.where((group == 3) & (col == row), diag, turned))
    return first, jnp.where(group == 1, first, turned)


def solve_pair(a, b, c, d):
    inverse = 1.0 / a
    lower = c * inverse
    inverse_rest = 1.0 / (d - lower * b)

    def solve(top, bottom):
        second = (bottom - lower * top) * inverse_rest
        return (top - b * second) * inverse, second

    return solve


def eliminate(work, step, at):
    rows = lax.broadcasted_iota(jnp.int32, work.shape, 0)
    cols = [jnp.broadcast_to(work[:, at + step + n : at + step + n + 1], work.shape) for n in range(4)]
    line = [work[step + n : step + n + 1, :] for n in range(4)]
    piv = [[cols[m][step + n : step + n + 1, :] for m in range(4)] for n in range(4)]
    first_block = solve_pair(piv[0][0], piv[0][1], piv[1][0], piv[1][1])
    new0, new1 = first_block(line[0], line[1])
    cross = [first_block(piv[0][m], piv[1][m]) for m in (2, 3)]
    rest = [[piv[n][m + 2] - piv[n][0] * cross[m][0] - piv[n][1] * cross[m][1] for m in range(2)] for n in (2, 3)]
    left2 = line[2] - piv[2][0] * new0 - piv[2][1] * new1
    left3 = line[3] - piv[3][0] * new0 - piv[3][1] * new1
    new2, new3 = solve_pair(rest[0][0], rest[0][1], rest[1][0], rest[1][1])(left2, left3)
    new0 = new0 - cross[0][0] * new2 - cross[1][0] * new3
    new1 = new1 - cross[0][1] * new2 - cross[1][1] * new3
    work = work - (cols[0] * new0 + cols[1] * new1) - (cols[2] * new2 + cols[3] * new3)
    for n, new in enumerate((new0, new1, new2, new3)):
        work = jnp.where(rows == step + n, new, work)
    return work


def final_kernel(mine_ref, other_ref, sol_ref, res_ref, dir_ref, image_ref, new_sol_ref, new_res_ref, new_dir_ref):
    rhs = sol_ref.shape[0]
    even = lax.axis_index("side") == 0
    quarters = [jnp.where(even, mine_ref[n], other_ref[n]) for n in range(3)]
    quarters += [jnp.where(even, other_ref[n], mine_ref[n]) for n in range(3)]
    first, second = unpack_gram([jnp.concatenate(quarters[2 * n : 2 * n + 2], axis=0) for n in range(3)])
    for step in range(0, rhs, 4):
        first = eliminate(first, step, 0)
        second = eliminate(second, step, rhs)
    alpha = first[:, 32:64]
    row = lax.broadcasted_iota(jnp.int32, (rhs, rhs), 0)
    col = lax.broadcasted_iota(jnp.int32, (rhs, rhs), 1)
    eye = (row == col).astype(F32)
    beta = eye - first[:, 64:96] + dot_f32(first[:, 96:128] - second[:, 64:96], alpha, ((1,), (0,)))
    direction = dir_ref[...]
    new_sol_ref[...] = sol_ref[...] + dot_f32(alpha, direction, ((0,), (0,)))
    new_res = res_ref[...] - dot_f32(alpha, image_ref[...], ((0,), (0,)))
    new_res_ref[...] = new_res
    new_dir_ref[...] = new_res + dot_f32(beta, direction, ((0,), (0,)))


def call(kernel, outs, ins, name, megabytes, scratch=(), space=pltpu.VMEM):
    return pl.pallas_call(
        kernel,
        out_shape=tuple(jax.ShapeDtypeStruct(*out) for out in outs),
        in_specs=[pl.BlockSpec(memory_space=space)] * len(ins),
        out_specs=(pl.BlockSpec(memory_space=pltpu.VMEM),) * len(outs),
        scratch_shapes=scratch,
        compiler_params=pltpu.CompilerParams(vmem_limit_bytes=megabytes << 20),
        name=name,
    )(*ins)


def per_device(chips, points, noise_var, district, solution, residual, direction):
    rhs, count = direction.shape
    whole_count = count * chips * 2
    group = ("row", "pair")
    swap = [(0, 1), (1, 0)]
    wide = ((rhs, count), F32)
    fetched = (points, district.reshape(1, count), noise_var.reshape(1, count), direction)
    fetched = tuple(pltpu.with_memory_space_constraint(arg, pltpu.HBM) for arg in fetched)
    block, own = call(
        pack_kernel,
        (((ROWS, LANES), BF16), ((8, count), F32)),
        fetched,
        "pack", 4,
        [pltpu.VMEM(arg.shape, arg.dtype) for arg in fetched] + [pltpu.SemaphoreType.DMA((len(fetched),))],
        pltpu.HBM,
    )
    cores = [list(range(0, 2 * chips, 2)), [(n + chips) % (2 * chips) + 1 for n in range(0, 2 * chips, 2)]]
    near = lax.all_to_all(
        jnp.broadcast_to(block[None], (chips, ROWS, LANES)), group + ("side",), 0, 0, axis_index_groups=cores
    )
    far = lax.ppermute(near, "side", swap)
    product, sums, norm, side = call(
        first_kernel,
        (wide, ((rhs + 8, count), F32), ((rhs, LANES), F32), ((count, 40), BF16)),
        (own, direction, residual, near),
        "near_half", 24,
    )
    image, packed = call(
        functools.partial(second_kernel, whole_count),
        (wide, ((6, 4, LANES), F32)),
        (own, direction, residual, norm, product, sums, side, far),
        "far_half", 24,
    )
    copies = jnp.broadcast_to(packed.reshape(1, 2, 3, 4, LANES), (chips, 2, 3, 4, LANES)).reshape(-1, 3, 4, LANES)
    mine = jnp.sum(lax.all_to_all(copies, group + ("side",), 0, 0, tiled=True), axis=0)
    other = lax.ppermute(mine, "side", swap)
    return call(
        final_kernel,
        (wide,) * 3,
        (mine, other, solution, residual, direction, image),
        "final", 8,
    )


def solution(mesh):
    rows, cols = mesh.shape["row"], mesh.shape["col"]
    paired = Mesh(mesh.devices.reshape(rows, cols // 2, 2), ("row", "pair", "side"))
    samples = ("row", "pair", "side")
    wide, flat = P(None, samples), P(samples)
    return jax.shard_map(
        functools.partial(per_device, rows * cols // 2),
        mesh=paired,
        in_specs=(wide, flat, flat, wide, wide, wide),
        out_specs=(wide, wide, wide),
        check_vma=False,
    )
```

```python
import functools
import math

import jax
import jax.numpy as jnp
from jax import lax
from jax.experimental import pallas as pl
from jax.experimental.pallas import tpu as pltpu
from jax.sharding import Mesh, PartitionSpec as P

root_three = math.sqrt(3.0)
corr_range = 0.05
district_gain = 0.5
LANES = 128
ROWS = 72
F32, BF16 = jnp.float32, jnp.bfloat16


def dot_f32(left, right, dims):
    return lax.dot_general(
        left, right, (dims, ((), ())), precision=lax.Precision.HIGHEST, preferred_element_type=F32
    )


def dot_bf16(left, right, dims):
    return lax.dot_general(left, right, (dims, ((), ())), preferred_element_type=F32)


def three_pieces(vals):
    high = vals.astype(BF16)
    rest = vals - high.astype(F32)
    mid = rest.astype(BF16)
    low = (rest - mid.astype(F32)).astype(BF16)
    return high, mid, low


def stack_pieces(vals):
    rows, count = vals.shape
    ones = jnp.ones((LANES - 3 * rows, count), BF16)
    return jnp.concatenate([*three_pieces(vals), ones], axis=0)


def pack_kernel(
    points_hbm, dist_hbm, noise_hbm, dir_hbm, pack_ref, own_ref, points_ref, dist_ref, noise_ref, dir_ref, sems
):
    pairs = ((dir_hbm, dir_ref), (dist_hbm, dist_ref), (points_hbm, points_ref), (noise_hbm, noise_ref))
    copies = [pltpu.make_async_copy(src, dst, sems.at[n]) for n, (src, dst) in enumerate(pairs)]
    for copy in copies:
        copy.start()
    rhs, count = dir_ref.shape
    copies[1].wait()
    dist = dist_ref[...]
    first = dist[:, 0:1]
    last = dist[:, count - 1 : count]
    row = lax.broadcasted_iota(jnp.int32, (8, count), 0)
    picked = jnp.where(row == 0, first, last)
    wanted = (row == 0) | ((row == 1) & (first != last))
    mask = (wanted & (dist == picked)).astype(F32).astype(BF16)
    for copy in (copies[0], copies[2], copies[3]):
        copy.wait()
    pts = points_ref[...].astype(F32)
    own_ref[...] = jnp.concatenate(
        [pts, dist.astype(F32), noise_ref[...], jnp.zeros((4, count), F32)], axis=0
    )
    high, mid, low = three_pieces(dir_ref[...])
    ones = jnp.ones((LANES - 3 * rhs, count), BF16)
    edge = dot_bf16(mask, jnp.concatenate([high, high, high, ones], axis=0), ((1,), (1,)))
    edge = edge + dot_bf16(mask, jnp.concatenate([mid, mid, mid, 0 * ones], axis=0), ((1,), (1,)))
    edge = edge + dot_bf16(mask, jnp.concatenate([low, low, low, 0 * ones], axis=0), ((1,), (1,)))
    e_high, e_mid, e_low = (piece.astype(F32) for piece in three_pieces(edge))
    lane = lax.broadcasted_iota(jnp.int32, (8, LANES), 1)
    row8 = lax.broadcasted_iota(jnp.int32, (8, LANES), 0)
    label = jnp.where(row8 == 0, first, last).astype(F32)
    extras = jnp.where(lane < rhs, e_high, jnp.where(lane < 2 * rhs, e_mid, e_low))
    extras = jnp.where(lane == 3 * rhs, label, jnp.where(lane > 3 * rhs, edge, extras))
    tail = jnp.concatenate(
        [pts[:, 0:LANES], pts[:, LANES:], extras[0:2, :], jnp.zeros((2, LANES), F32)], axis=0
    )
    pack_ref[0:rhs, :] = high[:, 0:LANES]
    pack_ref[rhs : 2 * rhs, :] = high[:, LANES:]
    pack_ref[2 * rhs :, :] = tail.astype(BF16)


def own_side(own):
    scale = 3.0 / corr_range**2
    row = lax.broadcasted_iota(jnp.int32, own.shape, 0)
    cross = jnp.where(row < 2, own * (-2.0 * scale), 0.0)
    square = own * own
    norm = scale * (square[0:1] + square[1:2])
    cross_high, cross_low, _ = three_pieces(cross)
    high, mid, low = (piece.astype(F32) for piece in three_pieces(norm))
    ones = jnp.where(row < 2, scale, 0.0)
    norms = jnp.where(row == 0, high, jnp.where(row == 1, mid, jnp.where(row == 2, low, 0.0)))
    return jnp.concatenate([cross_high.astype(F32), cross_low.astype(F32), ones, ones, norms], axis=0)


def other_side(tail):
    left = tail.astype(F32)
    right = pltpu.roll(left, left.shape[0] - 2, 0)
    coords = jnp.concatenate([left, right], axis=1)
    square = coords * coords
    high = square.astype(BF16).astype(F32)
    return jnp.concatenate([coords, coords, high, square - high, jnp.ones_like(coords)], axis=0).astype(BF16)


def half_product(skip, own_ref, all_ref, side):
    blocks = all_ref.shape[0]
    count = own_ref.shape[1]
    rhs = 32
    to_two = -math.log2(math.e)

    def one_block(index, acc):
        block = all_ref[index]
        square = dot_bf16(side[...], other_side(block[2 * rhs :, :]), ((1,), (0,)))
        square = jnp.maximum(square, 1e-30)
        scaled = square * lax.rsqrt(square)
        tile = ((1.0 + scaled) * jnp.exp2(scaled * to_two)).astype(BF16)
        left = jnp.concatenate([block[0:rhs, :], block[rhs : 2 * rhs, :]], axis=1)
        return acc + dot_bf16(left, tile, ((1,), (1,)))

    def some_blocks(index, acc):
        for inner in range(batch):
            acc = one_block(index * batch + inner, acc)
        return acc

    batch = math.gcd(blocks, 16)
    product = jnp.zeros((rhs, count), F32)
    if blocks == batch:
        product = some_blocks(0, product)
    else:
        product = lax.fori_loop(0, blocks // batch, some_blocks, product)

    edges = all_ref[:, 2 * rhs :, :].astype(F32).reshape(blocks * 8, LANES)
    place = lax.broadcasted_iota(jnp.int32, (blocks * 8, count), 0)
    kind = place % 8
    good = ((kind == 4) | (kind == 5)) & (place // 8 != skip)
    match = good & (edges[:, 3 * rhs : 3 * rhs + 1] == own_ref[2:3, :])
    sums = dot_bf16(edges.astype(BF16), match.astype(F32).astype(BF16), ((0,), (0,)))
    extra = sums[0:rhs] + sums[rhs : 2 * rhs] + sums[2 * rhs : 3 * rhs]
    return product, extra, sums[3 * rhs + 1 : 3 * rhs + 2]


def place_in_group(chips):
    place = lax.axis_index(("row", "pair"))
    return jnp.where(lax.axis_index("side") == 0, place, (place + 3 * chips // 4) % chips)


def first_kernel(own_ref, dir_ref, res_ref, all_ref, product_ref, sums_ref, norm_ref, side_ref):
    rhs, count = dir_ref.shape
    side_ref[...] = own_side(own_ref[...]).T.astype(BF16)
    product, extra, number = half_product(place_in_group(all_ref.shape[0]), own_ref, all_ref, side_ref)
    product_ref[...] = product
    labels = lax.broadcasted_iota(jnp.int32, (64, count), 0).astype(F32)
    onehot = (labels == own_ref[2:3, :]).astype(F32).astype(BF16)
    same = dot_bf16(onehot, onehot, ((0,), (0,))).astype(BF16)
    sums = dot_bf16(stack_pieces(dir_ref[...]), same, ((1,), (0,)))
    sums_ref[0:rhs, :] = sums[0:rhs] + sums[rhs : 2 * rhs] + sums[2 * rhs : 3 * rhs] + extra
    sums_ref[rhs:, :] = sums[3 * rhs : 3 * rhs + 8] + number
    residual = res_ref[...]
    norm_ref[...] = jnp.zeros_like(norm_ref)
    norm_ref[:, 32:64] = dot_f32(residual, residual, ((1,), (1,)))


def second_kernel(
    whole_count, own_ref, dir_ref, res_ref, norm_ref, product_ref, sums_ref, side_ref, all_ref,
    image_ref, packed_ref,
):
    product, extra, number = half_product(-1, own_ref, all_ref, side_ref)
    product = product + product_ref[...]
    size = sums_ref[32:33, :] + number
    district_part = (sums_ref[0:32, :] + extra) / jnp.sqrt(size)
    direction = dir_ref[...]
    kernel_scale = 1.0 / (corr_range * math.sqrt(whole_count))
    image = own_ref[3:4, :] * direction + product * kernel_scale + district_gain * district_part
    image_ref[...] = image
    part = 0.5 * direction
    none = jnp.zeros_like(part)
    gram = dot_f32(image, jnp.concatenate([part, none, res_ref[...], image], axis=0), ((1,), (1,)))
    gram = gram + dot_f32(part, jnp.concatenate([image, none, none, none], axis=0), ((1,), (1,)))
    gram = gram + norm_ref[...]
    packed = pack_gram(gram)
    for n in range(6):
        packed_ref[n] = packed[n // 2][4 * (n % 2) : 4 * (n % 2) + 4, :]


def lane_groups(height):
    row = lax.broadcasted_iota(jnp.int32, (height, LANES), 0)
    lane = lax.broadcasted_iota(jnp.int32, (height, LANES), 1)
    return row, lane % 32, lane // 32


def pack_gram(gram):
    row, col, group = lane_groups(32)
    below = (col <= row) & (group <= 1)
    kept = jnp.where(below | (group == 2) | ((group == 3) & (col > row)), gram, 0.0)
    diag = jnp.sum(jnp.where((group == 3) & (col == row), gram, 0.0), axis=0, keepdims=True)
    diag = jnp.broadcast_to(diag, (8, LANES))
    row8, col8, group8 = lane_groups(8)
    packed = [jnp.zeros((8, LANES), F32)] * 3
    for n in range(4):
        rows = kept[8 * n : 8 * n + 8]
        for source, target in ((0, 1), (1, 2), (2, 0), (3, 1)):
            turn = (n - source) % 4 * 32
            moved = pltpu.roll(rows, turn, 1) if turn else rows
            packed[target] = packed[target] + jnp.where(group8 == n, moved, 0.0)
    packed[2] = packed[2] + jnp.where((group8 == 0) & (row8 == 0) & (col8 > 0), pltpu.roll(diag, 32, 1), 0.0)
    packed[2] = packed[2] + jnp.where((group8 == 0) & (row8 == 1) & (col8 == 2), pltpu.roll(diag, 34, 1), 0.0)
    return packed


def unpack_gram(packed):
    _, _, group8 = lane_groups(8)
    parts = []
    for n in range(4):
        rows = jnp.zeros((8, LANES), F32)
        for source, target in ((0, 1), (1, 2), (2, 0), (3, 1)):
            turn = (source - n) % 4 * 32
            moved = pltpu.roll(packed[target], turn, 1) if turn else packed[target]
            rows = jnp.where(group8 == source, moved, rows)
        parts.append(rows)
    flat = jnp.concatenate(parts, axis=0)
    row, col, group = lane_groups(32)
    spread = jnp.concatenate([jnp.where(group == n, flat, 0.0) for n in range(4)], axis=0).T
    turned = (spread[0:32] + spread[32:64]) + (spread[64:96] + spread[96:128])
    diag = jnp.where(col[0:1] == 0, pltpu.roll(flat[0:8], 62, 1)[1:2], pltpu.roll(flat[0:8], 64, 1)[0:1])
    direct = (group == 2) | ((group <= 1) & (col <= row)) | ((group == 3) & (col > row))
    first = jnp.where(direct, flat, jnp.where((group == 3) & (col == row), diag, turned))
    return first, jnp.where(group == 1, first, turned)


def solve_pair(a, b, c, d):
    inverse = 1.0 / a
    lower = c * inverse
    inverse_rest = 1.0 / (d - lower * b)

    def solve(top, bottom):
        second = (bottom - lower * top) * inverse_rest
        return (top - b * second) * inverse, second

    return solve


def eliminate(work, step, at):
    rows = lax.broadcasted_iota(jnp.int32, work.shape, 0)
    cols = [jnp.broadcast_to(work[:, at + step + n : at + step + n + 1], work.shape) for n in range(4)]
    line = [work[step + n : step + n + 1, :] for n in range(4)]
    piv = [[cols[m][step + n : step + n + 1, :] for m in range(4)] for n in range(4)]
    first_block = solve_pair(piv[0][0], piv[0][1], piv[1][0], piv[1][1])
    new0, new1 = first_block(line[0], line[1])
    cross = [first_block(piv[0][m], piv[1][m]) for m in (2, 3)]
    rest = [[piv[n][m + 2] - piv[n][0] * cross[m][0] - piv[n][1] * cross[m][1] for m in range(2)] for n in (2, 3)]
    left2 = line[2] - piv[2][0] * new0 - piv[2][1] * new1
    left3 = line[3] - piv[3][0] * new0 - piv[3][1] * new1
    new2, new3 = solve_pair(rest[0][0], rest[0][1], rest[1][0], rest[1][1])(left2, left3)
    new0 = new0 - cross[0][0] * new2 - cross[1][0] * new3
    new1 = new1 - cross[0][1] * new2 - cross[1][1] * new3
    work = work - (cols[0] * new0 + cols[1] * new1) - (cols[2] * new2 + cols[3] * new3)
    for n, new in enumerate((new0, new1, new2, new3)):
        work = jnp.where(rows == step + n, new, work)
    return work


def spread_left(vals):
    high, mid, low = (piece.astype(F32) for piece in three_pieces(vals))
    return jnp.concatenate([high, high, mid, high, mid, low], axis=0).astype(BF16)


def spread_right(vals):
    high, mid, low = three_pieces(vals)
    return jnp.concatenate([high, mid, high, low, mid, high], axis=0)


def final_kernel(mine_ref, other_ref, sol_ref, res_ref, dir_ref, image_ref, new_sol_ref, new_res_ref, new_dir_ref):
    rhs = sol_ref.shape[0]
    even = lax.axis_index("side") == 0
    quarters = [jnp.where(even, mine_ref[n], other_ref[n]) for n in range(3)]
    quarters += [jnp.where(even, other_ref[n], mine_ref[n]) for n in range(3)]
    first, second = unpack_gram([jnp.concatenate(quarters[2 * n : 2 * n + 2], axis=0) for n in range(3)])
    for step in range(0, rhs, 4):
        first = eliminate(first, step, 0)
        second = eliminate(second, step, rhs)
    alpha = first[:, 32:64]
    row = lax.broadcasted_iota(jnp.int32, (rhs, rhs), 0)
    col = lax.broadcasted_iota(jnp.int32, (rhs, rhs), 1)
    eye = (row == col).astype(F32)
    beta = eye - first[:, 64:96] + dot_f32(first[:, 96:128] - second[:, 64:96], alpha, ((1,), (0,)))
    direction, image = spread_right(dir_ref[...]), spread_right(image_ref[...])
    spread_alpha = spread_left(alpha)
    new_sol_ref[...] = sol_ref[...] + dot_bf16(spread_alpha, direction, ((0,), (0,)))
    new_res = res_ref[...] - dot_bf16(spread_alpha, image, ((0,), (0,)))
    new_res_ref[...] = new_res
    new_dir_ref[...] = new_res + dot_bf16(spread_left(beta), direction, ((0,), (0,)))


def call(kernel, outs, ins, name, megabytes, scratch=(), space=pltpu.VMEM):
    return pl.pallas_call(
        kernel,
        out_shape=tuple(jax.ShapeDtypeStruct(*out) for out in outs),
        in_specs=[pl.BlockSpec(memory_space=space)] * len(ins),
        out_specs=(pl.BlockSpec(memory_space=pltpu.VMEM),) * len(outs),
        scratch_shapes=scratch,
        compiler_params=pltpu.CompilerParams(vmem_limit_bytes=megabytes << 20),
        name=name,
    )(*ins)


def per_device(chips, points, noise_var, district, solution, residual, direction):
    rhs, count = direction.shape
    whole_count = count * chips * 2
    group = ("row", "pair")
    swap = [(0, 1), (1, 0)]
    wide = ((rhs, count), F32)
    fetched = (points, district.reshape(1, count), noise_var.reshape(1, count), direction)
    fetched = tuple(pltpu.with_memory_space_constraint(arg, pltpu.HBM) for arg in fetched)
    block, own = call(
        pack_kernel,
        (((ROWS, LANES), BF16), ((8, count), F32)),
        fetched,
        "pack", 4,
        [pltpu.VMEM(arg.shape, arg.dtype) for arg in fetched] + [pltpu.SemaphoreType.DMA((len(fetched),))],
        pltpu.HBM,
    )
    cores = [list(range(0, 2 * chips, 2)), [(n + chips // 2) % (2 * chips) + 1 for n in range(0, 2 * chips, 2)]]
    near = lax.all_to_all(
        jnp.broadcast_to(block[None], (chips, ROWS, LANES)), group + ("side",), 0, 0, axis_index_groups=cores
    )
    far = lax.ppermute(near, "side", swap)
    product, sums, norm, side = call(
        first_kernel,
        (wide, ((rhs + 8, count), F32), ((rhs, LANES), F32), ((count, 40), BF16)),
        (own, direction, residual, near),
        "near_half", 24,
    )
    image, packed = call(
        functools.partial(second_kernel, whole_count),
        (wide, ((6, 4, LANES), F32)),
        (own, direction, residual, norm, product, sums, side, far),
        "far_half", 24,
    )
    copies = jnp.broadcast_to(packed.reshape(1, 2, 3, 4, LANES), (chips, 2, 3, 4, LANES)).reshape(-1, 3, 4, LANES)
    mine = jnp.sum(lax.all_to_all(copies, group + ("side",), 0, 0, tiled=True), axis=0)
    other = lax.ppermute(mine, "side", swap)
    return call(
        final_kernel,
        (wide,) * 3,
        (mine, other, solution, residual, direction, image),
        "final", 8,
    )


def solution(mesh):
    rows, cols = mesh.shape["row"], mesh.shape["col"]
    paired = Mesh(mesh.devices.reshape(rows, cols // 2, 2), ("row", "pair", "side"))
    samples = ("row", "pair", "side")
    wide, flat = P(None, samples), P(samples)
    return jax.shard_map(
        functools.partial(per_device, rows * cols // 2),
        mesh=paired,
        in_specs=(wide, flat, flat, wide, wide, wide),
        out_specs=(wide, wide, wide),
        check_vma=False,
    )
```
